256 devices in a mesh: seq: 16 (over z_lo, x), hid: 16 (over z_hi, y, core).
Axes of the slice: x: 4, y: 4, z: 8 (z_hi: 2, z_lo: 4; z = z_hi * 4 + z_lo), core: 2. Of those that a mesh axis runs over, the one named last changes fastest.
Arguments:
- tokens: bfloat16 [65536, 2048], P('seq', 'hid'), may hold values from -6 to 6
- cotangent: bfloat16 [65536, 2048], P('seq', 'hid'), may hold values from -6 to 6
- seq_first: bfloat16 [128, 512, 512], P('seq'), may hold values from -0.25 to 0.25
- seq_second: bfloat16 [512, 128, 128], P('seq'), may hold values from -0.5 to 0.5
- feat_first: bfloat16 [32, 64, 64], P('hid'), may hold values from -0.75 to 0.75
- feature_second_blocks: bfloat16 [64, 32, 32], P('hid'), may hold values from -1 to 1
- gate_scale: float32 [2048], P('hid'), may hold values from 0.5 to 2
- gate_bias: float32 [2048], P('hid'), may hold values from -3 to 3
Outputs:
- result: bfloat16 [65536, 2048], P('seq', 'hid')
- token_grad: bfloat16 [65536, 2048], P('seq', 'hid')
- first_grad: float32 [128, 512, 512], P('seq', 'hid')
- second_grad: float32 [512, 128, 128], P('seq', 'hid')
The draws below stay inside these ranges and needn't reach their ends.
All inputs are finite; a program needn't handle non-finite values.
Results may differ from the reference program's by a relative error of at most 0.0061.
Values may be sent and summed in bfloat16 or wider, within the bound.
No kernel may reach another device: no remote copies, remote signals or barrier semaphores. Data moves between devices by JAX's collectives and lax.ppermute only.
A program may use at most 128 MiB of HBM per device.

```python
import jax
import jax.numpy as jnp

SB = 512
NB = 128
FB = 64
NF = 32
TOKENS = 65536
D = 2048


def levels(rng, shape, split, smallest, top_value):
    level, own = 1.0, jax.random.fold_in(rng, 6)
    for axis_at, shards_of in split:
        heights = jnp.exp(jax.random.uniform(jax.random.fold_in(own, axis_at), (shards_of,), jnp.float32, smallest / len(split), top_value / len(split)))
        level = level * jnp.repeat(heights, shape[axis_at] // shards_of).reshape([-1 if axis == axis_at else 1 for axis in range(len(shape))])
    return level


def bell_draw(key, extent, scale, bound, shards=(), held_as=jnp.bfloat16):
    factor_of = levels(key, extent, shards, -0.22, 0.18) if shards else 1.0
    values = jax.random.normal(key, extent, jnp.float32) * scale * factor_of
    return jnp.minimum(jnp.maximum(values, -bound), bound).astype(held_as)


def setup_inputs(seed: int = 0) -> dict:
    keys = jax.random.split(jax.random.key(seed), 9)
    return {
        "tokens": bell_draw(keys[0], (TOKENS, D), 1.0, 6.0, ((0, 16), (1, 16))),
        "cotangent": bell_draw(keys[1], (TOKENS, D), 1.0, 6.0, ((0, 16), (1, 16))),
        "seq_first": bell_draw(keys[2], (NB, SB, SB), SB ** -0.5, 0.25, ((0, 16),)),
        "seq_second": bell_draw(keys[3], (SB, NB, NB), NB ** -0.5, 0.5, ((0, 16),)),
        "feat_first": bell_draw(keys[4], (NF, FB, FB), FB ** -0.5, 0.75, ((0, 16),)),
        "feature_second_blocks": bell_draw(keys[5], (FB, NF, NF), NF ** -0.5, 1.0, ((0, 16),)),
        "gate_scale": jnp.clip(0.5 + 1.5 * jax.random.uniform(keys[6], (D,), jnp.float32) ** levels(keys[6], (D,), ((0, 16),), -0.2, 0.2), 0.5, 2.0),
        "gate_bias": bell_draw(keys[7], (D,), 1.0, 3.0, ((0, 16),), jnp.float32),
    }


def gelu_slope(value):
    normal_cdf = 0.5 * (1.0 + jax.scipy.special.erf(value * 0.7071067811865476))
    density = jnp.exp(-0.5 * value * value) * 0.3989422804014327
    return normal_cdf + value * density


def reference(tokens, cotangent, seq_first, seq_second, feat_first, feature_second_blocks, gate_scale, gate_bias):
    widened_input = jnp.float32
    half = jnp.bfloat16
    x_blocks = tokens.reshape(NB, SB, D).astype(widened_input)
    first = jnp.einsum('qkj,qjc->qkc', seq_first.astype(widened_input), x_blocks).astype(half)
    first_t = first.transpose(1, 0, 2).astype(widened_input)
    mixed_t = jnp.einsum('jab,jbc->jac', seq_second.astype(widened_input), first_t).astype(half)
    mixed = mixed_t.transpose(1, 0, 2).reshape(TOKENS, D).astype(widened_input)
    x_wide = tokens.astype(widened_input)
    gate = jax.nn.sigmoid(x_wide * gate_scale + gate_bias)
    hidden_state = (x_wide + gate * mixed).astype(half)
    panels = hidden_state.reshape(TOKENS, NF, FB).astype(widened_input)
    inner = jnp.einsum('bio,tbo->tbi', feat_first.astype(widened_input), panels).astype(half)
    activation_values = jax.nn.gelu(inner.astype(widened_input), approximate=False).astype(half)
    outer = jnp.einsum('ibd,tdi->tbi', feature_second_blocks.astype(widened_input), activation_values.astype(widened_input)).astype(half)
    result = (hidden_state.astype(widened_input) + outer.reshape(TOKENS, D).astype(widened_input)).astype(half)
    cot_panels = cotangent.reshape(TOKENS, NF, FB).astype(widened_input)
    activation_gradient = jnp.einsum('ibd,tbi->tdi', feature_second_blocks.astype(widened_input), cot_panels)
    d_inner = (activation_gradient * gelu_slope(inner.astype(widened_input))).astype(half)
    d_hidden = cotangent.astype(widened_input) + jnp.einsum('bio,tbi->tbo', feat_first.astype(widened_input), d_inner.astype(widened_input)).reshape(TOKENS, D)
    d_mixed = (d_hidden * gate).astype(half)
    d_mixed_t = d_mixed.reshape(NB, SB, D).transpose(1, 0, 2).astype(widened_input)
    d_first_t = jnp.einsum('jab,jac->jbc', seq_second.astype(widened_input), d_mixed_t).astype(half)
    second_grad = jnp.einsum('jac,jbc->jab', d_mixed_t, first_t)
    d_first = d_first_t.transpose(1, 0, 2).astype(widened_input)
    first_grad = jnp.einsum('qkc,qjc->qkj', d_first, x_blocks)
    seq_part = jnp.einsum('qkj,qkc->qjc', seq_first.astype(widened_input), d_first).reshape(TOKENS, D)
    local_part = d_hidden * (1.0 + gate_scale * gate * (1.0 - gate) * mixed)
    token_grad = (seq_part + local_part).astype(half)
    return result, token_grad, first_grad, second_grad
```

```python
import jax
import jax.numpy as jnp
from jax import lax
from jax.sharding import Mesh
from jax.sharding import PartitionSpec as P

CHUNKS = 1
SEQ = ("zl", "x")
HID = ("zh", "y", "c")
PLANE = ("y", "c")
F32 = jnp.float32
BF16 = jnp.bfloat16


def swap(value, axes):
    return lax.all_to_all(value, axes, split_axis=0, concat_axis=0, tiled=True)


def gelu_slope(value):
    normal_cdf = 0.5 * (1.0 + jax.scipy.special.erf(value * 0.7071067811865476))
    density = jnp.exp(-0.5 * value * value) * 0.3989422804014327
    return normal_cdf + value * density


def dot(spec, left, right):
    return jnp.einsum(spec, left, right, preferred_element_type=F32)


def spread_second(blocks):
    group, panels = blocks.shape[0], blocks.shape[1]
    width = group * panels
    rows = blocks.transpose(2, 0, 1).reshape(width, panels)
    col = lax.broadcasted_iota(jnp.int32, (panels, width), 1)
    pick = (col // group == lax.broadcasted_iota(jnp.int32, (panels, width), 0)).astype(BF16)
    full = dot("rb,bn->rn", rows, pick)
    at = lax.broadcasted_iota(jnp.int32, (width, width), 0) % group
    to = lax.broadcasted_iota(jnp.int32, (width, width), 1) % group
    return jnp.where(at == to, full, 0.0).astype(BF16)


def on_device(
    tokens,
    cotangent,
    seq_first,
    seq_second,
    feat_first,
    feature_second_blocks,
    gate_scale,
    gate_bias,
):
    n_seq, n_hid = lax.axis_size(SEQ), lax.axis_size(HID)
    n_plane = lax.axis_size(PLANE)
    zh = lax.axis_index("zh")
    rows, width = tokens.shape
    blocks, block = seq_first.shape[0], seq_first.shape[1]
    offs, nb = seq_second.shape[0], seq_second.shape[1]
    groups, group = feat_first.shape[0], feat_first.shape[1]
    per = offs // CHUNKS

    x_blocks = tokens.reshape(blocks, block, width)
    order = (n_seq, CHUNKS, per, blocks, width)
    x_rows = x_blocks.transpose(1, 0, 2).reshape(order)
    cot_rows = cotangent.reshape(blocks, block, width).transpose(1, 0, 2).reshape(order)
    second = seq_second.reshape(CHUNKS, per, nb, nb)

    eye = jnp.eye(groups, dtype=BF16)
    panel = (feat_first[:, :, None, :] * eye[:, None, :, None]).reshape(width, width)

    first = dot("qkj,qjc->kqc", seq_first, x_blocks).astype(BF16).reshape(order)
    x_plane = swap(x_blocks, PLANE).reshape(n_plane, block, width)
    spread = spread_second(lax.all_gather(feature_second_blocks, HID, axis=0, tiled=True))
    spread = spread.reshape(n_hid, width, n_hid, width)

    results, locals_, firsts, second_grads, first_grads = [], [], [], [], []
    for ch in range(CHUNKS):
        strided = swap(first[:, ch], SEQ).transpose(1, 0, 2, 3).reshape(per, nb, width)
        mixed_j = dot("jab,jbc->jac", second[ch], strided).astype(BF16)
        mixed_j = mixed_j.reshape(per, n_seq, blocks, width).transpose(1, 0, 2, 3)
        mixed = swap(mixed_j, SEQ).astype(F32)
        x_wide = x_rows[:, ch].astype(F32)
        cot = cot_rows[:, ch]
        gate = jax.nn.sigmoid(x_wide * gate_scale + gate_bias)
        hidden = (x_wide + gate * mixed).astype(BF16)
        inner = dot("sjqo,io->sjqi", hidden, panel).astype(BF16)
        by_row = (n_hid, per * blocks * n_seq // n_hid, width)
        cot_moved = swap(cot.reshape(by_row), HID)
        inner_moved = swap(inner.reshape(by_row), HID)
        inner_wide = inner_moved.astype(F32)
        act = jax.nn.gelu(inner_wide, approximate=False).astype(BF16)
        outer = dot("htc,hcdn->dtn", act, spread).astype(BF16)
        d_act = dot("dtn,hcdn->htc", cot_moved, spread)
        d_inner = (d_act * gelu_slope(inner_wide)).astype(BF16)
        d_back = swap(d_inner, HID).reshape(hidden.shape)
        d_hidden = cot.astype(F32) + dot("sjqi,io->sjqo", d_back, panel)
        d_mixed = (d_hidden * gate).astype(BF16)
        locals_.append(d_hidden * (1.0 + gate_scale * gate * (1.0 - gate) * mixed))
        d_mixed_j = swap(d_mixed, SEQ).transpose(1, 0, 2, 3).reshape(per, nb, width)
        d_first_j = dot("jab,jac->jbc", second[ch], d_mixed_j).astype(BF16)
        d_first_j = d_first_j.reshape(per, n_seq, blocks, width).transpose(1, 0, 2, 3)
        firsts.append(swap(d_first_j, SEQ))

        outer = swap(outer, HID).reshape(hidden.shape)
        results.append((hidden.astype(F32) + outer.astype(F32)).astype(BF16))

        part = dot("jac,jbc->jab", d_mixed_j, strided).astype(BF16)
        part = part.reshape(per, n_hid // n_plane, n_plane, nb // n_hid, nb)
        part = swap(part.transpose(2, 1, 0, 3, 4), PLANE)
        part = part.reshape(n_plane, n_hid // n_plane, per, nb // n_hid, nb).astype(F32).sum(0)
        keep = lax.dynamic_index_in_dim(part, zh, 0, keepdims=False)
        send = lax.dynamic_index_in_dim(part, 1 - zh, 0, keepdims=False)
        second_grads.append(keep + lax.ppermute(send, "zh", [(0, 1), (1, 0)]))

        d_first_q = firsts[ch].transpose(2, 0, 1, 3).reshape(blocks, n_seq * per, width)
        d_plane = swap(d_first_q, PLANE).reshape(n_plane, n_seq * per, width)
        prod = dot("skc,sjc->kj", d_plane, x_plane)
        prod = prod.reshape(n_hid // n_plane, n_plane, per, block)
        keep = lax.dynamic_index_in_dim(prod, zh, 0, keepdims=False)
        send = lax.dynamic_index_in_dim(prod, 1 - zh, 0, keepdims=False).astype(BF16)
        prod = keep + lax.ppermute(send, "zh", [(0, 1), (1, 0)]).astype(F32)
        first_grads.append(swap(prod, PLANE))

    def whole(parts):
        stacked = jnp.stack(parts, axis=1)
        return stacked.reshape(block, blocks, width).transpose(1, 0, 2).reshape(rows, width)

    d_first = jnp.stack(firsts, axis=1).reshape(block, blocks, width)
    seq_part = dot("qkj,kqc->qjc", seq_first, d_first).reshape(rows, width)
    token_grad = (seq_part + whole(locals_)).astype(BF16)
    first_grad = jnp.concatenate(first_grads, axis=1)
    second_grad = jnp.concatenate(second_grads, axis=0)
    return whole(results), token_grad, first_grad, second_grad


def solution(mesh):
    fine = Mesh(mesh.devices.reshape(4, 4, 2, 4, 2), ("zl", "x", "zh", "y", "c"))
    return jax.shard_map(
        on_device,
        mesh=fine,
        in_specs=(
            P(SEQ, HID),
            P(SEQ, HID),
            P(SEQ, None, None),
            P(SEQ, None, None),
            P(HID, None, None),
            P(HID, None, None),
            P(HID),
            P(HID),
        ),
        out_specs=(P(SEQ, HID), P(SEQ, HID), P(SEQ, HID, None), P(SEQ, HID, None)),
        check_vma=False,
    )
```

```python
import jax
import jax.numpy as jnp
from jax import lax
from jax.experimental import pallas as pl
from jax.sharding import Mesh
from jax.sharding import PartitionSpec as P

SEQ = ("zl", "x")
HID = ("zh", "y", "c")
PLANE = ("y", "c")
F32 = jnp.float32
BF16 = jnp.bfloat16


def move(value, axes):
    return lax.all_to_all(value, axes, split_axis=0, concat_axis=0, tiled=True)


def turn(value, axis, dim):
    size, me = lax.axis_size(axis), lax.axis_index(axis)
    got = []
    for r in range(1, size):
        part = lax.dynamic_index_in_dim(value, me ^ r, dim, keepdims=True)
        got.append(lax.ppermute(part, axis, [(s, s ^ r) for s in range(size)]))
    for r in range(1, size):
        value = lax.dynamic_update_slice_in_dim(value, got[r - 1], me ^ r, dim)
    return value


def swap(value, axes):
    shape = value.shape
    value = value.reshape(tuple(lax.axis_size(a) for a in axes) + shape[1:])
    for dim, axis in enumerate(axes):
        value = turn(value, axis, dim)
    return value.reshape(shape)


def dot(spec, left, right):
    return jnp.einsum(spec, left, right, preferred_element_type=F32)


def mix_kernel(inner_ref, cot_ref, rows_ref, outer_ref, d_inner_ref):
    panels, offs, count = inner_ref.shape
    width = panels * offs
    col = lax.broadcasted_iota(jnp.int32, (panels, width), 1)
    row = lax.broadcasted_iota(jnp.int32, (panels, width), 0)
    pick = (col // offs == row).astype(F32).astype(BF16)
    full = jnp.dot(rows_ref[...].reshape(width, panels), pick, preferred_element_type=F32)
    at = lax.broadcasted_iota(jnp.int32, (width, width), 0) % offs
    to = lax.broadcasted_iota(jnp.int32, (width, width), 1) % offs
    spread = jnp.where(at == to, full, 0.0).astype(BF16)
    d_act = jnp.dot(spread, cot_ref[...].reshape(width, count), preferred_element_type=F32)
    inner = inner_ref[...].reshape(width, count).astype(F32)
    cdf = 0.5 * (1.0 + lax.erf(inner * 0.7071067811865476))
    density = jnp.exp(-0.5 * inner * inner) * 0.3989422804014327
    d_inner = (d_act * (cdf + inner * density)).astype(BF16)
    d_inner_ref[...] = d_inner.reshape(panels, offs, count)
    act = (inner * cdf).astype(BF16)
    outer = lax.dot_general(
        spread, act, (((0,), (0,)), ((), ())), preferred_element_type=F32
    ).astype(BF16)
    outer_ref[...] = outer.reshape(panels, offs, count)


def mix_features(inner, cot, blocks):
    panels, group, count = inner.shape
    offs = 16
    rows = blocks.transpose(2, 0, 1)
    data = pl.BlockSpec((panels, offs, count), lambda g: (0, g, 0))
    return pl.pallas_call(
        mix_kernel,
        out_shape=(jax.ShapeDtypeStruct(inner.shape, BF16),) * 2,
        grid=(group // offs,),
        in_specs=[data, data, pl.BlockSpec((panels, offs, panels), lambda g: (0, g, 0))],
        out_specs=(data, data),
        name="mix_features",
    )(inner, cot, rows)


def steps(
    tokens,
    cotangent,
    seq_first,
    seq_second,
    feat_first,
    feature_second_blocks,
    gate_scale,
    gate_bias,
):
    n_seq, n_hid = lax.axis_size(SEQ), lax.axis_size(HID)
    n_plane = lax.axis_size(PLANE)
    halves = n_hid // n_plane
    zh = lax.axis_index("zh")
    rows, width = tokens.shape
    blocks, block = seq_first.shape[0], seq_first.shape[1]
    offs, nb = seq_second.shape[0], seq_second.shape[1]
    groups, group = feat_first.shape[0], feat_first.shape[1]
    panels = feature_second_blocks.shape[1]
    count = rows // n_hid
    wide = (n_hid, count, width)
    tall = (n_hid, width, count)
    flat = (n_seq, offs, blocks, width)
    by_panel = (panels, group, count)

    x_blocks = tokens.reshape(blocks, block, width)
    first = dot("qkj,qjc->kqc", seq_first, x_blocks).astype(BF16).reshape(flat)
    first = move(first, SEQ)

    x_rows = x_blocks.transpose(1, 0, 2).reshape(wide)
    cot_rows = cotangent.reshape(blocks, block, width).transpose(1, 0, 2).reshape(wide)
    small = feature_second_blocks.reshape(1, -1, count)
    small = jnp.broadcast_to(small, (n_hid,) + small.shape[1:])
    sent = jnp.concatenate([cot_rows.transpose(0, 2, 1), small], axis=1)
    eye = jnp.eye(groups, dtype=BF16)
    panel = (feat_first[:, :, None, :] * eye[:, None, :, None]).reshape(width, width)
    panel = jnp.broadcast_to(panel, (n_hid, width, width))
    got = swap(sent, HID)
    x_plane = swap(x_blocks, PLANE)
    cot_moved = got[:, :width].reshape(by_panel)
    second_all = got[:, width:].reshape(group, panels, panels)

    strided = first.transpose(1, 0, 2, 3).reshape(offs, nb, width)
    mixed_j = dot("jab,jbc->jac", seq_second, strided).astype(BF16)
    mixed_j = mixed_j.reshape(offs, n_seq, blocks, width).transpose(1, 0, 2, 3)
    mixed = move(mixed_j, SEQ).reshape(wide)
    mixed = mixed.astype(F32)
    x_wide = x_rows.astype(F32)
    gate = jax.nn.sigmoid(x_wide * gate_scale + gate_bias)
    hidden = (x_wide + gate * mixed).astype(BF16)
    inner = dot("sio,sro->sir", panel, hidden).astype(BF16)
    inner_moved = move(inner, HID).reshape(by_panel)
    outer, d_inner = mix_features(inner_moved, cot_moved, second_all)
    d_back = move(d_inner.reshape(tall), HID)
    outer = swap(outer.reshape(tall), HID).transpose(0, 2, 1)
    d_hidden = cot_rows.astype(F32) + dot("sir,sio->sro", d_back, panel)
    d_mixed = (d_hidden * gate).astype(BF16)
    local = d_hidden * (1.0 + gate_scale * gate * (1.0 - gate) * mixed)
    d_mixed = move(d_mixed.reshape(flat), SEQ)
    d_mixed_j = d_mixed.transpose(1, 0, 2, 3).reshape(offs, nb, width)
    d_first_j = dot("jab,jac->jbc", seq_second, d_mixed_j).astype(BF16)
    d_first_j = d_first_j.reshape(offs, n_seq, blocks, width).transpose(1, 0, 2, 3)
    d_first = move(d_first_j, SEQ).reshape(block, blocks, width)

    part = dot("jac,jbc->jab", d_mixed_j, strided).astype(BF16)
    part = part.reshape(offs, halves, n_plane, nb // n_hid, nb)
    part = swap(part.transpose(2, 1, 0, 3, 4), PLANE)
    part = part.astype(F32).sum(0)
    keep = lax.dynamic_index_in_dim(part, zh, 0, keepdims=False)
    send = lax.dynamic_index_in_dim(part, 1 - zh, 0, keepdims=False)
    second_grad = keep + lax.ppermute(send, "zh", [(0, 1), (1, 0)])

    d_first_q = d_first.transpose(1, 0, 2)
    d_plane = move(d_first_q, PLANE)
    prod = dot("skc,sjc->kj", d_plane, x_plane).astype(BF16)
    prod = move(prod.reshape(n_hid, offs, block), HID)
    prod = prod.reshape(halves, n_plane, offs, block).astype(F32)
    first_grad = prod[0] + prod[1]

    def whole(value):
        return value.reshape(block, blocks, width).transpose(1, 0, 2).reshape(rows, width)

    result = whole((hidden.astype(F32) + outer.astype(F32)).astype(BF16))
    seq_part = dot("qkj,qkc->qjc", seq_first, d_first_q).reshape(rows, width)
    token_grad = (seq_part + whole(local)).astype(BF16)
    return result, token_grad, first_grad, second_grad


def solution(mesh):
    fine = Mesh(mesh.devices.reshape(4, 4, 2, 4, 2), ("zl", "x", "zh", "y", "c"))
    return jax.shard_map(
        steps,
        mesh=fine,
        in_specs=(
            P(SEQ, HID),
            P(SEQ, HID),
            P(SEQ, None, None),
            P(SEQ, None, None),
            P(HID, None, None),
            P(HID, None, None),
            P(HID),
            P(HID),
        ),
        out_specs=(P(SEQ, HID), P(SEQ, HID), P(SEQ, HID, None), P(SEQ, HID, None)),
        check_vma=False,
    )
```

```python
import jax
import jax.numpy as jnp
from jax import lax
from jax.experimental import pallas as pl
from jax.sharding import Mesh
from jax.sharding import PartitionSpec as P

SEQ = ("zl", "x")
HID = ("zh", "y", "c")
PLANE = ("y", "c")
F32 = jnp.float32
BF16 = jnp.bfloat16


def move(value, axes):
    return lax.all_to_all(value, axes, split_axis=0, concat_axis=0, tiled=True)


def turn(value, axis, dim):
    size, me = lax.axis_size(axis), lax.axis_index(axis)
    parts = [
        lax.dynamic_index_in_dim(value, me ^ r, dim, keepdims=True) for r in range(1, size)
    ]
    value, *parts = lax.optimization_barrier((value, *parts))
    got = []
    for r in range(1, size):
        got.append(lax.ppermute(parts[r - 1], axis, [(s, s ^ r) for s in range(size)]))
    for r in range(1, size):
        value = lax.dynamic_update_slice_in_dim(value, got[r - 1], me ^ r, dim)
    return value


def swap(value, axes):
    shape = value.shape
    value = value.reshape(tuple(lax.axis_size(a) for a in axes) + shape[1:])
    for dim, axis in enumerate(axes):
        value = turn(value, axis, dim)
    return value.reshape(shape)


def dot(spec, left, right):
    return jnp.einsum(spec, left, right, preferred_element_type=F32)


def mix_kernel(inner_ref, cot_ref, rows_ref, outer_ref, d_inner_ref):
    panels, offs, count = inner_ref.shape
    width = panels * offs
    col = lax.broadcasted_iota(jnp.int32, (panels, width), 1)
    row = lax.broadcasted_iota(jnp.int32, (panels, width), 0)
    pick = (col // offs == row).astype(F32).astype(BF16)
    full = jnp.dot(rows_ref[...].reshape(width, panels), pick, preferred_element_type=F32)
    at = lax.broadcasted_iota(jnp.int32, (width, width), 0) % offs
    to = lax.broadcasted_iota(jnp.int32, (width, width), 1) % offs
    spread = jnp.where(at == to, full, 0.0).astype(BF16)
    d_act = jnp.dot(spread, cot_ref[...].reshape(width, count), preferred_element_type=F32)
    inner = inner_ref[...].reshape(width, count).astype(F32)
    cdf = 0.5 * (1.0 + lax.erf(inner * 0.7071067811865476))
    density = jnp.exp(-0.5 * inner * inner) * 0.3989422804014327
    d_inner = (d_act * (cdf + inner * density)).astype(BF16)
    d_inner_ref[...] = d_inner.reshape(panels, offs, count)
    act = (inner * cdf).astype(BF16)
    outer = lax.dot_general(
        spread, act, (((0,), (0,)), ((), ())), preferred_element_type=F32
    ).astype(BF16)
    outer_ref[...] = outer.reshape(panels, offs, count)


def mix_features(inner, cot, blocks):
    panels, group, count = inner.shape
    offs = 16
    rows = blocks.transpose(2, 0, 1)
    data = pl.BlockSpec((panels, offs, count), lambda g: (0, g, 0))
    return pl.pallas_call(
        mix_kernel,
        out_shape=(jax.ShapeDtypeStruct(inner.shape, BF16),) * 2,
        grid=(group // offs,),
        in_specs=[data, data, pl.BlockSpec((panels, offs, panels), lambda g: (0, g, 0))],
        out_specs=(data, data),
        name="mix_features",
    )(inner, cot, rows)


def gated(x_ref, mixed_ref, scale_ref, bias_ref):
    x = x_ref[...].astype(F32)
    mixed = mixed_ref[...].astype(F32)
    return x, mixed, jax.nn.sigmoid(x * scale_ref[...] + bias_ref[...])


def enter_kernel(x_ref, mixed_ref, scale_ref, bias_ref, panel_ref, hidden_ref, inner_ref):
    x, mixed, gate = gated(x_ref, mixed_ref, scale_ref, bias_ref)
    hidden_ref[...] = (x + gate * mixed).astype(BF16)
    for k in range(x_ref.shape[0]):
        inner = lax.dot_general(
            panel_ref[...],
            hidden_ref[k],
            (((1,), (1,)), ((), ())),
            preferred_element_type=F32,
        )
        inner_ref[k] = inner.astype(BF16)


def back_kernel(
    x_ref, mixed_ref, scale_ref, bias_ref, panel_ref, cot_ref, d_ref, d_mixed_ref, local_ref
):
    _, mixed, gate = gated(x_ref, mixed_ref, scale_ref, bias_ref)
    slope = 1.0 + scale_ref[...] * gate * (1.0 - gate) * mixed
    for k in range(x_ref.shape[0]):
        d_hidden = cot_ref[k].astype(F32) + lax.dot_general(
            d_ref[k],
            panel_ref[...],
            (((0,), (0,)), ((), ())),
            preferred_element_type=F32,
        )
        d_mixed_ref[k] = (d_hidden * gate[k]).astype(BF16)
        local_ref[k] = d_hidden * slope[k]


def by_rows(kernel, x, mixed, scale, bias, panel, more, outs):
    owners, _, width = x.shape
    here = 4

    def spec(shape):
        return pl.BlockSpec((here,) + shape[1:], lambda g: (g, 0, 0))

    vector = pl.BlockSpec((1, width), lambda g: (0, 0))
    return pl.pallas_call(
        kernel,
        out_shape=outs,
        grid=(owners // here,),
        in_specs=[spec(x.shape), spec(x.shape), vector, vector]
        + [pl.BlockSpec((width, width), lambda g: (0, 0))]
        + [spec(m.shape) for m in more],
        out_specs=tuple(spec(o.shape) for o in outs),
    )(x, mixed, scale.reshape(1, width), bias.reshape(1, width), panel, *more)


def steps(
    tokens,
    cotangent,
    seq_first,
    seq_second,
    feat_first,
    feature_second_blocks,
    gate_scale,
    gate_bias,
):
    n_seq, n_hid = lax.axis_size(SEQ), lax.axis_size(HID)
    n_plane = lax.axis_size(PLANE)
    halves = n_hid // n_plane
    zh = lax.axis_index("zh")
    rows, width = tokens.shape
    blocks, block = seq_first.shape[0], seq_first.shape[1]
    offs, nb = seq_second.shape[0], seq_second.shape[1]
    groups, group = feat_first.shape[0], feat_first.shape[1]
    panels = feature_second_blocks.shape[1]
    count = rows // n_hid
    wide = (n_hid, count, width)
    tall = (n_hid, width, count)
    flat = (n_seq, offs, blocks, width)
    by_panel = (panels, group, count)

    x_blocks = tokens.reshape(blocks, block, width)
    first = dot("qkj,qjc->kqc", seq_first, x_blocks).astype(BF16).reshape(flat)
    first = move(first, SEQ)

    x_rows = x_blocks.transpose(1, 0, 2).reshape(wide)
    cot_rows = cotangent.reshape(blocks, block, width).transpose(1, 0, 2).reshape(wide)
    small = feature_second_blocks.reshape(1, -1, count)
    small = jnp.broadcast_to(small, (n_hid,) + small.shape[1:])
    sent = jnp.concatenate([cot_rows.transpose(0, 2, 1), small], axis=1)
    eye = jnp.eye(groups, dtype=BF16)
    panel = (feat_first[:, :, None, :] * eye[:, None, :, None]).reshape(width, width)
    got = swap(sent, HID)
    x_plane = swap(x_blocks, PLANE)
    cot_moved = got[:, :width].reshape(by_panel)
    second_all = got[:, width:].reshape(group, panels, panels)

    strided = first.transpose(1, 0, 2, 3).reshape(offs, nb, width)
    mixed_j = dot("jab,jbc->jac", seq_second, strided).astype(BF16)
    mixed_j = mixed_j.reshape(offs, n_seq, blocks, width).transpose(1, 0, 2, 3)
    mixed = move(mixed_j, SEQ).reshape(wide)
    hidden, inner = by_rows(
        enter_kernel,
        x_rows,
        mixed,
        gate_scale,
        gate_bias,
        panel,
        (),
        (jax.ShapeDtypeStruct(wide, BF16), jax.ShapeDtypeStruct(tall, BF16)),
    )
    inner_moved = move(inner, HID).reshape(by_panel)
    outer, d_inner = mix_features(inner_moved, cot_moved, second_all)
    d_back = move(d_inner.reshape(tall), HID)
    outer = swap(outer.reshape(tall), HID).transpose(0, 2, 1)
    d_mixed, local = by_rows(
        back_kernel,
        x_rows,
        mixed,
        gate_scale,
        gate_bias,
        panel,
        (cot_rows, d_back),
        (jax.ShapeDtypeStruct(wide, BF16), jax.ShapeDtypeStruct(wide, F32)),
    )
    d_mixed = move(d_mixed.reshape(flat), SEQ)
    d_mixed_j = d_mixed.transpose(1, 0, 2, 3).reshape(offs, nb, width)
    d_first_j = dot("jab,jac->jbc", seq_second, d_mixed_j).astype(BF16)
    d_first_j = d_first_j.reshape(offs, n_seq * blocks, width).transpose(1, 0, 2)
    d_first = move(d_first_j, SEQ + PLANE).reshape(n_seq, n_plane, offs, width)

    part = dot("jac,jbc->jab", d_mixed_j, strided).astype(BF16)
    part = part.reshape(offs, halves, n_plane, nb // n_hid, nb)
    part = swap(part.transpose(2, 1, 0, 3, 4), PLANE)
    part = part.astype(F32).sum(0)
    keep = lax.dynamic_index_in_dim(part, zh, 0, keepdims=False)
    send = lax.dynamic_index_in_dim(part, 1 - zh, 0, keepdims=False)
    second_grad = keep + lax.ppermute(send, "zh", [(0, 1), (1, 0)])

    prod = dot("spjc,pkc->sjk", d_first, x_plane).astype(BF16)
    prod = move(prod.reshape(n_hid, offs, block), HID)
    prod = prod.reshape(halves, n_plane, offs, block).astype(F32)
    first_grad = prod[0] + prod[1]

    own = lax.dynamic_index_in_dim(seq_first, lax.axis_index(PLANE), 0, keepdims=False)
    own = own.reshape(n_seq, offs, block)
    seq_part = dot("sjk,spjc->pkc", own, d_first).astype(BF16)
    seq_part = swap(seq_part, PLANE).reshape(rows, width)

    def whole(value):
        return value.reshape(block, blocks, width).transpose(1, 0, 2).reshape(rows, width)

    result = whole((hidden.astype(F32) + outer.astype(F32)).astype(BF16))
    local = whole(local)
    token_grad = (seq_part.astype(F32) + local).astype(BF16)
    return result, token_grad, first_grad, second_grad


def solution(mesh):
    fine = Mesh(mesh.devices.reshape(4, 4, 2, 4, 2), ("zl", "x", "zh", "y", "c"))
    return jax.shard_map(
        steps,
        mesh=fine,
        in_specs=(
            P(SEQ, HID),
            P(SEQ, HID),
            P(SEQ, None, None),
            P(SEQ, None, None),
            P(HID, None, None),
            P(HID, None, None),
            P(HID),
            P(HID),
        ),
        out_specs=(P(SEQ, HID), P(SEQ, HID), P(SEQ, HID, None), P(SEQ, HID, None)),
        check_vma=False,
    )
```

```python
import jax
import jax.numpy as jnp
from jax import lax
from jax.experimental import pallas as pl
from jax.sharding import Mesh
from jax.sharding import PartitionSpec as P

SEQ = ("zl", "x")
HID = ("zh", "y", "c")
PLANE = ("y", "c")
F32 = jnp.float32
BF16 = jnp.bfloat16


def move(value, axes):
    return lax.all_to_all(value, axes, split_axis=0, concat_axis=0, tiled=True)


def turn(value, axis, dim):
    size, me = lax.axis_size(axis), lax.axis_index(axis)
    parts = [
        lax.dynamic_index_in_dim(value, me ^ r, dim, keepdims=True) for r in range(1, size)
    ]
    if size > 2:
        parts = lax.optimization_barrier(parts)
    got = []
    for r in range(1, size):
        got.append(lax.ppermute(parts[r - 1], axis, [(s, s ^ r) for s in range(size)]))
    for r in range(1, size):
        value = lax.dynamic_update_slice_in_dim(value, got[r - 1], me ^ r, dim)
    return value


def swap(value, axes):
    shape = value.shape
    value = value.reshape(tuple(lax.axis_size(a) for a in axes) + shape[1:])
    for dim, axis in enumerate(axes):
        value = turn(value, axis, dim)
    return value.reshape(shape)


def dot(spec, left, right):
    return jnp.einsum(spec, left, right, preferred_element_type=F32)


def mix_kernel(inner_ref, cot_ref, rows_ref, outer_ref, d_inner_ref):
    panels, offs, count = inner_ref.shape
    width = panels * offs
    col = lax.broadcasted_iota(jnp.int32, (panels, width), 1)
    row = lax.broadcasted_iota(jnp.int32, (panels, width), 0)
    pick = (col // offs == row).astype(F32).astype(BF16)
    full = jnp.dot(rows_ref[...].reshape(width, panels), pick, preferred_element_type=F32)
    at = lax.broadcasted_iota(jnp.int32, (width, width), 0) % offs
    to = lax.broadcasted_iota(jnp.int32, (width, width), 1) % offs
    spread = jnp.where(at == to, full, 0.0).astype(BF16)
    d_act = jnp.dot(spread, cot_ref[...].reshape(width, count), preferred_element_type=F32)
    inner = inner_ref[...].reshape(width, count).astype(F32)
    cdf = 0.5 * (1.0 + lax.erf(inner * 0.7071067811865476))
    density = jnp.exp(-0.5 * inner * inner) * 0.3989422804014327
    d_inner = (d_act * (cdf + inner * density)).astype(BF16)
    d_inner_ref[...] = d_inner.reshape(panels, offs, count)
    act = (inner * cdf).astype(BF16)
    outer = lax.dot_general(
        spread, act, (((0,), (0,)), ((), ())), preferred_element_type=F32
    ).astype(BF16)
    outer_ref[...] = outer.reshape(panels, offs, count)


def mix_features(inner, cot, blocks):
    panels, group, count = inner.shape
    offs = 16
    rows = blocks.transpose(2, 0, 1)
    data = pl.BlockSpec((panels, offs, count), lambda g: (0, g, 0))
    return pl.pallas_call(
        mix_kernel,
        out_shape=(jax.ShapeDtypeStruct(inner.shape, BF16),) * 2,
        grid=(group // offs,),
        in_specs=[data, data, pl.BlockSpec((panels, offs, panels), lambda g: (0, g, 0))],
        out_specs=(data, data),
        name="mix_features",
    )(inner, cot, rows)


def gated(x_ref, mixed_ref, scale_ref, bias_ref):
    x = x_ref[...].astype(F32)
    mixed = mixed_ref[...].astype(F32)
    return x, mixed, jax.nn.sigmoid(x * scale_ref[...] + bias_ref[...])


def enter_kernel(x_ref, mixed_ref, scale_ref, bias_ref, panel_ref, hidden_ref, inner_ref):
    x, mixed, gate = gated(x_ref, mixed_ref, scale_ref, bias_ref)
    hidden_ref[...] = (x + gate * mixed).astype(BF16)
    for k in range(x_ref.shape[0]):
        inner = lax.dot_general(
            panel_ref[...],
            hidden_ref[k],
            (((1,), (1,)), ((), ())),
            preferred_element_type=F32,
        )
        inner_ref[k] = inner.astype(BF16)


def back_kernel(
    x_ref, mixed_ref, scale_ref, bias_ref, panel_ref, cot_ref, d_ref, d_mixed_ref, local_ref
):
    _, mixed, gate = gated(x_ref, mixed_ref, scale_ref, bias_ref)
    slope = 1.0 + scale_ref[...] * gate * (1.0 - gate) * mixed
    for k in range(x_ref.shape[0]):
        d_hidden = cot_ref[k].astype(F32) + lax.dot_general(
            d_ref[k],
            panel_ref[...],
            (((0,), (0,)), ((), ())),
            preferred_element_type=F32,
        )
        d_mixed_ref[k] = (d_hidden * gate[k]).astype(BF16)
        local_ref[k] = d_hidden * slope[k]


def by_rows(kernel, x, mixed, scale, bias, panel, more, outs):
    owners, _, width = x.shape
    here = 4

    def spec(shape):
        return pl.BlockSpec((here,) + shape[1:], lambda g: (g, 0, 0))

    vector = pl.BlockSpec((1, width), lambda g: (0, 0))
    return pl.pallas_call(
        kernel,
        out_shape=outs,
        grid=(owners // here,),
        in_specs=[spec(x.shape), spec(x.shape), vector, vector]
        + [pl.BlockSpec((width, width), lambda g: (0, 0))]
        + [spec(m.shape) for m in more],
        out_specs=tuple(spec(o.shape) for o in outs),
    )(x, mixed, scale.reshape(1, width), bias.reshape(1, width), panel, *more)


def finish_kernel(part_ref, local_ref, out_ref):
    out_ref[...] = (part_ref[...].astype(F32) + local_ref[...]).astype(BF16)


def finish(part, local):
    rows, width = part.shape
    block = pl.BlockSpec((rows // 4, width), lambda g: (g, 0))
    return pl.pallas_call(
        finish_kernel,
        out_shape=jax.ShapeDtypeStruct(part.shape, BF16),
        grid=(4,),
        in_specs=[block, block],
        out_specs=block,
        name="finish",
    )(part, local)


def steps(
    tokens,
    cotangent,
    seq_first,
    seq_second,
    feat_first,
    feature_second_blocks,
    gate_scale,
    gate_bias,
):
    n_seq, n_hid = lax.axis_size(SEQ), lax.axis_size(HID)
    n_plane = lax.axis_size(PLANE)
    halves = n_hid // n_plane
    zh = lax.axis_index("zh")
    rows, width = tokens.shape
    blocks, block = seq_first.shape[0], seq_first.shape[1]
    offs, nb = seq_second.shape[0], seq_second.shape[1]
    groups, group = feat_first.shape[0], feat_first.shape[1]
    panels = feature_second_blocks.shape[1]
    count = rows // n_hid
    wide = (n_hid, count, width)
    tall = (n_hid, width, count)
    flat = (n_seq, offs, blocks, width)
    by_panel = (panels, group, count)

    x_blocks = tokens.reshape(blocks, block, width)
    first = dot("qkj,qjc->kqc", seq_first, x_blocks).astype(BF16).reshape(flat)
    first = move(first, SEQ)

    x_rows = x_blocks.transpose(1, 0, 2).reshape(wide)
    cot_rows = cotangent.reshape(blocks, block, width).transpose(1, 0, 2).reshape(wide)
    small = feature_second_blocks.reshape(1, -1, count)
    small = jnp.broadcast_to(small, (n_hid,) + small.shape[1:])
    sent = jnp.concatenate([cot_rows.transpose(0, 2, 1), small], axis=1)
    eye = jnp.eye(groups, dtype=BF16)
    panel = (feat_first[:, :, None, :] * eye[:, None, :, None]).reshape(width, width)
    got = swap(sent, HID)
    x_plane = swap(x_blocks, PLANE)
    cot_moved = got[:, :width].reshape(by_panel)
    second_all = got[:, width:].reshape(group, panels, panels)

    strided = first.transpose(1, 0, 2, 3).reshape(offs, nb, width)
    mixed_j = dot("jab,jbc->jac", seq_second, strided).astype(BF16)
    mixed_j = mixed_j.reshape(offs, n_seq, blocks, width).transpose(1, 0, 2, 3)
    mixed = move(mixed_j, SEQ).reshape(wide)
    hidden, inner = by_rows(
        enter_kernel,
        x_rows,
        mixed,
        gate_scale,
        gate_bias,
        panel,
        (),
        (jax.ShapeDtypeStruct(wide, BF16), jax.ShapeDtypeStruct(tall, BF16)),
    )
    inner_moved = move(inner, HID).reshape(by_panel)
    outer, d_inner = mix_features(inner_moved, cot_moved, second_all)
    d_back = move(d_inner.reshape(tall), HID)
    outer = swap(outer.reshape(tall), HID).transpose(0, 2, 1)
    d_mixed, local = by_rows(
        back_kernel,
        x_rows,
        mixed,
        gate_scale,
        gate_bias,
        panel,
        (cot_rows, d_back),
        (jax.ShapeDtypeStruct(wide, BF16), jax.ShapeDtypeStruct(wide, F32)),
    )
    d_mixed = move(d_mixed.reshape(flat), SEQ)
    d_mixed_j = d_mixed.transpose(1, 0, 2, 3).reshape(offs, nb, width)
    d_first_j = dot("jab,jac->jbc", seq_second, d_mixed_j).astype(BF16)
    d_first_j = d_first_j.reshape(offs, n_seq * blocks, width).transpose(1, 0, 2)
    d_first = move(d_first_j, SEQ + PLANE).reshape(n_seq, n_plane, offs, width)

    part = dot("jac,jbc->jab", d_mixed_j, strided).astype(BF16)
    part = part.reshape(offs, halves, n_plane, nb // n_hid, nb)
    part = swap(part.transpose(2, 1, 0, 3, 4), PLANE)
    part = part.astype(F32).sum(0)
    keep = lax.dynamic_index_in_dim(part, zh, 0, keepdims=False)
    send = lax.dynamic_index_in_dim(part, 1 - zh, 0, keepdims=False)
    second_grad = keep + lax.ppermute(send, "zh", [(0, 1), (1, 0)])

    prod = dot("spjc,pkc->sjk", d_first, x_plane).astype(BF16)
    prod = move(prod.reshape(n_hid, offs, block), HID)
    prod = prod.reshape(halves, n_plane, offs, block).astype(F32)
    first_grad = prod[0] + prod[1]

    own = lax.dynamic_index_in_dim(seq_first, lax.axis_index(PLANE), 0, keepdims=False)
    own = own.reshape(n_seq, offs, block)
    seq_part = dot("sjk,spjc->pkc", own, d_first).astype(BF16)
    seq_part = swap(seq_part, PLANE).reshape(rows, width)

    def whole(value):
        return value.reshape(block, blocks, width).transpose(1, 0, 2).reshape(rows, width)

    result = whole((hidden.astype(F32) + outer.astype(F32)).astype(BF16))
    local = whole(local)
    token_grad = finish(seq_part, local)
    return result, token_grad, first_grad, second_grad


def solution(mesh):
    fine = Mesh(mesh.devices.reshape(4, 4, 2, 4, 2), ("zl", "x", "zh", "y", "c"))
    return jax.shard_map(
        steps,
        mesh=fine,
        in_specs=(
            P(SEQ, HID),
            P(SEQ, HID),
            P(SEQ, None, None),
            P(SEQ, None, None),
            P(HID, None, None),
            P(HID, None, None),
            P(HID),
            P(HID),
        ),
        out_specs=(P(SEQ, HID), P(SEQ, HID), P(SEQ, HID, None), P(SEQ, HID, None)),
        check_vma=False,
    )
```

```python
import jax
import jax.numpy as jnp
from jax import lax
from jax.experimental import pallas as pl
from jax.experimental.pallas import tpu as pltpu
from jax.sharding import Mesh
from jax.sharding import PartitionSpec as P

SEQ = ("zl", "x")
HID = ("zh", "y", "c")
PLANE = ("y", "c")
F32 = jnp.float32
BF16 = jnp.bfloat16


def move(value, axes):
    return lax.all_to_all(value, axes, split_axis=0, concat_axis=0, tiled=True)


def trade(value, axis, dim):
    size, me = lax.axis_size(axis), lax.axis_index(axis)
    parts = [
        lax.dynamic_index_in_dim(value, me ^ r, dim, keepdims=True) for r in range(1, size)
    ]
    if size > 2:
        parts = lax.optimization_barrier(parts)
    got = []
    for r in range(1, size):
        got.append(lax.ppermute(parts[r - 1], axis, [(s, s ^ r) for s in range(size)]))
    return got


def fold(value, axis, dim):
    got = trade(value, axis, dim)
    total = lax.dynamic_index_in_dim(value, lax.axis_index(axis), dim).astype(F32)
    for part in got:
        total = total + part.astype(F32)
    return total.squeeze(dim)


def gather(value, axis):
    size, me = lax.axis_size(axis), lax.axis_index(axis)
    whole = jnp.zeros((size,) + value.shape, value.dtype)
    whole = lax.dynamic_update_index_in_dim(whole, value, me, 0)
    for r in range(1, size):
        other = lax.ppermute(value, axis, [(s, s ^ r) for s in range(size)])
        whole = lax.dynamic_update_index_in_dim(whole, other, me ^ r, 0)
    return whole


def turn(value, axis, dim):
    size, me = lax.axis_size(axis), lax.axis_index(axis)
    got = trade(value, axis, dim)
    for r in range(1, size):
        value = lax.dynamic_update_slice_in_dim(value, got[r - 1], me ^ r, dim)
    return value


def swap(value, axes):
    shape = value.shape
    value = value.reshape(tuple(lax.axis_size(a) for a in axes) + shape[1:])
    for dim, axis in enumerate(axes):
        value = turn(value, axis, dim)
    return value.reshape(shape)


def dot(spec, left, right):
    return jnp.einsum(spec, left, right, preferred_element_type=F32)


def mix_kernel(inner_ref, cot_ref, rows_ref, outer_ref, d_inner_ref):
    panels, offs, count = inner_ref.shape
    width = panels * offs
    col = lax.broadcasted_iota(jnp.int32, (panels, width), 1)
    row = lax.broadcasted_iota(jnp.int32, (panels, width), 0)
    pick = (col // offs == row).astype(F32).astype(BF16)
    full = jnp.dot(rows_ref[...].reshape(width, panels), pick, preferred_element_type=F32)
    at = lax.broadcasted_iota(jnp.int32, (width, width), 0) % offs
    to = lax.broadcasted_iota(jnp.int32, (width, width), 1) % offs
    spread = jnp.where(at == to, full, 0.0).astype(BF16)
    d_act = jnp.dot(spread, cot_ref[...].reshape(width, count), preferred_element_type=F32)
    inner = inner_ref[...].reshape(width, count).astype(F32)
    cdf = 0.5 * (1.0 + lax.erf(inner * 0.7071067811865476))
    density = jnp.exp(-0.5 * inner * inner) * 0.3989422804014327
    d_inner = (d_act * (cdf + inner * density)).astype(BF16)
    d_inner_ref[...] = d_inner.reshape(panels, offs, count)
    act = (inner * cdf).astype(BF16)
    outer = lax.dot_general(
        spread, act, (((0,), (0,)), ((), ())), preferred_element_type=F32
    ).astype(BF16)
    outer_ref[...] = outer.reshape(panels, offs, count)


def mix_features(inner, cot, blocks):
    panels, group, count = inner.shape
    offs = 16
    rows = blocks.transpose(2, 0, 1)
    data = pl.BlockSpec((panels, offs, count), lambda g: (0, g, 0))
    return pl.pallas_call(
        mix_kernel,
        out_shape=(jax.ShapeDtypeStruct(inner.shape, BF16),) * 2,
        grid=(group // offs,),
        in_specs=[data, data, pl.BlockSpec((panels, offs, panels), lambda g: (0, g, 0))],
        out_specs=(data, data),
        name="mix_features",
    )(inner, cot, rows)


def gated(x_ref, mixed_ref, scale_ref, bias_ref):
    x = x_ref[...].astype(F32)
    mixed = mixed_ref[...].astype(F32)
    return x, mixed, jax.nn.sigmoid(x * scale_ref[...] + bias_ref[...])


def enter_kernel(x_ref, mixed_ref, scale_ref, bias_ref, panel_ref, hidden_ref, inner_ref):
    x, mixed, gate = gated(x_ref, mixed_ref, scale_ref, bias_ref)
    hidden_ref[...] = (x + gate * mixed).astype(BF16)
    for k in range(x_ref.shape[0]):
        inner = lax.dot_general(
            panel_ref[...],
            hidden_ref[k],
            (((1,), (1,)), ((), ())),
            preferred_element_type=F32,
        )
        inner_ref[k] = inner.astype(BF16)


def back_kernel(
    x_ref, mixed_ref, scale_ref, bias_ref, panel_ref, cot_ref, d_ref, d_mixed_ref, local_ref
):
    _, mixed, gate = gated(x_ref, mixed_ref, scale_ref, bias_ref)
    slope = 1.0 + scale_ref[...] * gate * (1.0 - gate) * mixed
    for k in range(x_ref.shape[0]):
        d_hidden = cot_ref[k].astype(F32) + lax.dot_general(
            d_ref[k],
            panel_ref[...],
            (((0,), (0,)), ((), ())),
            preferred_element_type=F32,
        )
        d_mixed_ref[k] = (d_hidden * gate[k]).astype(BF16)
        local_ref[k] = d_hidden * slope[k]


def by_rows(kernel, x, mixed, scale, bias, panel, more, outs):
    owners, _, width = x.shape
    here = 4

    def spec(shape):
        return pl.BlockSpec((here,) + shape[1:], lambda g: (g, 0, 0))

    vector = pl.BlockSpec((1, width), lambda g: (0, 0))
    return pl.pallas_call(
        kernel,
        out_shape=outs,
        grid=(owners // here,),
        in_specs=[spec(x.shape), spec(x.shape), vector, vector]
        + [pl.BlockSpec((width, width), lambda g: (0, 0))]
        + [spec(m.shape) for m in more],
        out_specs=tuple(spec(o.shape) for o in outs),
    )(x, mixed, scale.reshape(1, width), bias.reshape(1, width), panel, *more)


def close_kernel(d_ref, own_ref, x_ref, prod_ref, part_ref, total):
    step, (owners, here, offs, width) = pl.program_id(0), d_ref.shape
    height = owners * offs
    d_wide = jnp.concatenate([d_ref[:, k].reshape(height, width) for k in range(here)], axis=1)
    x_wide = jnp.concatenate([x_ref[k] for k in range(here)], axis=1)
    more = lax.dot_general(
        d_wide, x_wide, (((1,), (1,)), ((), ())), preferred_element_type=F32
    )
    part = lax.dot_general(
        own_ref[...], d_wide, (((0,), (0,)), ((), ())), preferred_element_type=F32
    ).astype(BF16)
    for k in range(here):
        part_ref[k] = part[:, k * width : (k + 1) * width]

    @pl.when(step == 0)
    def _():
        total[...] = more

    @pl.when(step > 0)
    def _():
        total[...] += more

    @pl.when(step == pl.num_programs(0) - 1)
    def _():
        prod_ref[...] = total[...].astype(BF16)


def close(d_first, own, x_plane):
    owners, plane, offs, width = d_first.shape
    height, here = owners * offs, 2
    square = pl.BlockSpec((height, height), lambda g: (0, 0))
    slab = pl.BlockSpec((here, height, width), lambda g: (g, 0, 0))
    return pl.pallas_call(
        close_kernel,
        out_shape=(
            jax.ShapeDtypeStruct((height, height), BF16),
            jax.ShapeDtypeStruct((plane, height, width), BF16),
        ),
        grid=(plane // here,),
        in_specs=[
            pl.BlockSpec((owners, here, offs, width), lambda g: (0, g, 0, 0)),
            square,
            slab,
        ],
        out_specs=(square, slab),
        scratch_shapes=[pltpu.VMEM((height, height), F32)],
        name="close",
    )(d_first, own, x_plane)


def finish_kernel(part_ref, local_ref, out_ref):
    out_ref[...] = (part_ref[...].astype(F32) + local_ref[...]).astype(BF16)


def finish(part, local):
    rows, width = part.shape
    block = pl.BlockSpec((rows // 4, width), lambda g: (g, 0))
    return pl.pallas_call(
        finish_kernel,
        out_shape=jax.ShapeDtypeStruct(part.shape, BF16),
        grid=(4,),
        in_specs=[block, block],
        out_specs=block,
        name="finish",
    )(part, local)


def steps(
    tokens,
    cotangent,
    seq_first,
    seq_second,
    feat_first,
    feature_second_blocks,
    gate_scale,
    gate_bias,
):
    n_seq, n_hid = lax.axis_size(SEQ), lax.axis_size(HID)
    n_plane = lax.axis_size(PLANE)
    halves = n_hid // n_plane
    rows, width = tokens.shape
    blocks, block = seq_first.shape[0], seq_first.shape[1]
    offs, nb = seq_second.shape[0], seq_second.shape[1]
    groups, group = feat_first.shape[0], feat_first.shape[1]
    panels = feature_second_blocks.shape[1]
    count = rows // n_hid
    wide = (n_hid, count, width)
    tall = (n_hid, width, count)
    flat = (n_seq, offs, blocks, width)
    by_panel = (panels, group, count)

    x_blocks = tokens.reshape(blocks, block, width)
    first = dot("qkj,qjc->kqc", seq_first, x_blocks).astype(BF16).reshape(flat)
    first = move(first, SEQ)

    x_rows = x_blocks.transpose(1, 0, 2).reshape(wide)
    cot_rows = cotangent.reshape(blocks, block, width).transpose(1, 0, 2).reshape(wide)
    small = feature_second_blocks.reshape(-1, width)
    sent = cot_rows.transpose(0, 2, 1)
    eye = jnp.eye(groups, dtype=BF16)
    panel = (feat_first[:, :, None, :] * eye[:, None, :, None]).reshape(width, width)
    got = swap(sent, HID)
    x_plane = swap(x_blocks, PLANE)
    cot_moved = got.reshape(by_panel)
    for axis in ("c", "y", "zh"):
        small = gather(small, axis)
    second_all = small.reshape(group, panels, panels)

    strided = first.transpose(1, 0, 2, 3).reshape(offs, nb, width)
    mixed_j = dot("jab,jbc->jac", seq_second, strided).astype(BF16)
    mixed_j = mixed_j.reshape(offs, n_seq, blocks, width).transpose(1, 0, 2, 3)
    mixed = move(mixed_j, SEQ).reshape(wide)
    hidden, inner = by_rows(
        enter_kernel,
        x_rows,
        mixed,
        gate_scale,
        gate_bias,
        panel,
        (),
        (jax.ShapeDtypeStruct(wide, BF16), jax.ShapeDtypeStruct(tall, BF16)),
    )
    inner_moved = move(inner, HID).reshape(by_panel)
    outer, d_inner = mix_features(inner_moved, cot_moved, second_all)
    d_back = move(d_inner.reshape(tall), HID)
    outer = swap(outer.reshape(tall), HID).transpose(0, 2, 1)
    d_mixed, local = by_rows(
        back_kernel,
        x_rows,
        mixed,
        gate_scale,
        gate_bias,
        panel,
        (cot_rows, d_back),
        (jax.ShapeDtypeStruct(wide, BF16), jax.ShapeDtypeStruct(wide, F32)),
    )
    d_mixed = move(d_mixed.reshape(flat), SEQ)
    d_mixed_j = d_mixed.transpose(1, 0, 2, 3).reshape(offs, nb, width)
    d_first_j = dot("jab,jac->jbc", seq_second, d_mixed_j).astype(BF16)
    d_first_j = d_first_j.reshape(offs, n_seq * blocks, width).transpose(1, 0, 2)
    d_first = move(d_first_j, SEQ + PLANE).reshape(n_seq, n_plane, offs, width)

    part = dot("jac,jbc->jab", d_mixed_j, strided).astype(BF16)
    part = part.reshape(offs, halves, n_plane, nb // n_hid, nb).transpose(2, 1, 0, 3, 4)
    part = part.reshape((lax.axis_size("y"), lax.axis_size("c")) + part.shape[1:])
    part = fold(part, "c", 1).astype(BF16)
    part = fold(part, "y", 0)
    second_grad = fold(part, "zh", 0)

    own = lax.dynamic_index_in_dim(seq_first, lax.axis_index(PLANE), 0, keepdims=False)
    prod, seq_part = close(d_first, own, x_plane)
    seq_part = swap(seq_part, PLANE).reshape(rows, width)
    prod = move(prod.reshape(n_hid, offs, block), HID)
    first_grad = prod.reshape(halves, n_plane, offs, block).astype(F32).sum(0)

    def whole(value):
        return value.reshape(block, blocks, width).transpose(1, 0, 2).reshape(rows, width)

    result = whole((hidden.astype(F32) + outer.astype(F32)).astype(BF16))
    local = whole(local)
    token_grad = finish(seq_part, local)
    return result, token_grad, first_grad, second_grad


def solution(mesh):
    fine = Mesh(mesh.devices.reshape(4, 4, 2, 4, 2), ("zl", "x", "zh", "y", "c"))
    return jax.shard_map(
        steps,
        mesh=fine,
        in_specs=(
            P(SEQ, HID),
            P(SEQ, HID),
            P(SEQ, None, None),
            P(SEQ, None, None),
            P(HID, None, None),
            P(HID, None, None),
            P(HID),
            P(HID),
        ),
        out_specs=(P(SEQ, HID), P(SEQ, HID), P(SEQ, HID, None), P(SEQ, HID, None)),
        check_vma=False,
    )
```

```python
import jax
import jax.numpy as jnp
from jax import lax
from jax.experimental import pallas as pl
from jax.experimental.pallas import tpu as pltpu
from jax.sharding import Mesh
from jax.sharding import PartitionSpec as P

SEQ = ("zl", "x")
HID = ("zh", "y", "c")
PLANE = ("y", "c")
F32 = jnp.float32
BF16 = jnp.bfloat16


def move(value, axes):
    return lax.all_to_all(value, axes, split_axis=0, concat_axis=0, tiled=True)


def trade(value, axis, dim):
    size, me = lax.axis_size(axis), lax.axis_index(axis)
    parts = [
        lax.dynamic_index_in_dim(value, me ^ r, dim, keepdims=True) for r in range(1, size)
    ]
    if size > 2:
        parts = lax.optimization_barrier(parts)
    got = []
    for r in range(1, size):
        got.append(lax.ppermute(parts[r - 1], axis, [(s, s ^ r) for s in range(size)]))
    return got


def fold(value, axis, dim):
    got = trade(value, axis, dim)
    total = lax.dynamic_index_in_dim(value, lax.axis_index(axis), dim).astype(F32)
    for part in got:
        total = total + part.astype(F32)
    return total.squeeze(dim)


def gather(value, axis):
    size, me = lax.axis_size(axis), lax.axis_index(axis)
    whole = jnp.zeros((size,) + value.shape, value.dtype)
    whole = lax.dynamic_update_index_in_dim(whole, value, me, 0)
    for r in range(1, size):
        other = lax.ppermute(value, axis, [(s, s ^ r) for s in range(size)])
        whole = lax.dynamic_update_index_in_dim(whole, other, me ^ r, 0)
    return whole


def turn(value, axis, dim):
    size, me = lax.axis_size(axis), lax.axis_index(axis)
    got = trade(value, axis, dim)
    for r in range(1, size):
        value = lax.dynamic_update_slice_in_dim(value, got[r - 1], me ^ r, dim)
    return value


def swap(value, axes):
    shape = value.shape
    value = value.reshape(tuple(lax.axis_size(a) for a in axes) + shape[1:])
    for dim, axis in enumerate(axes):
        value = turn(value, axis, dim)
    return value.reshape(shape)


def dot(spec, left, right):
    return jnp.einsum(spec, left, right, preferred_element_type=F32)


def mix_kernel(inner_ref, cot_ref, rows_ref, outer_ref, d_inner_ref):
    panels, offs, count = inner_ref.shape
    width = panels * offs
    col = lax.broadcasted_iota(jnp.int32, (panels, width), 1)
    row = lax.broadcasted_iota(jnp.int32, (panels, width), 0)
    pick = (col // offs == row).astype(F32).astype(BF16)
    full = jnp.dot(rows_ref[...].reshape(width, panels), pick, preferred_element_type=F32)
    at = lax.broadcasted_iota(jnp.int32, (width, width), 0) % offs
    to = lax.broadcasted_iota(jnp.int32, (width, width), 1) % offs
    spread = jnp.where(at == to, full, 0.0).astype(BF16)
    d_act = jnp.dot(spread, cot_ref[...].reshape(width, count), preferred_element_type=F32)
    inner = inner_ref[...].reshape(width, count).astype(F32)
    cdf = 0.5 * (1.0 + lax.erf(inner * 0.7071067811865476))
    density = jnp.exp(-0.5 * inner * inner) * 0.3989422804014327
    d_inner = (d_act * (cdf + inner * density)).astype(BF16)
    d_inner_ref[...] = d_inner.reshape(panels, offs, count)
    act = (inner * cdf).astype(BF16)
    outer = lax.dot_general(
        spread, act, (((0,), (0,)), ((), ())), preferred_element_type=F32
    ).astype(BF16)
    outer_ref[...] = outer.reshape(panels, offs, count)


def mix_features(inner, cot, blocks):
    panels, group, count = inner.shape
    offs = 16
    rows = blocks.transpose(2, 0, 1)
    data = pl.BlockSpec((panels, offs, count), lambda g: (0, g, 0))
    return pl.pallas_call(
        mix_kernel,
        out_shape=(jax.ShapeDtypeStruct(inner.shape, BF16),) * 2,
        grid=(group // offs,),
        in_specs=[data, data, pl.BlockSpec((panels, offs, panels), lambda g: (0, g, 0))],
        out_specs=(data, data),
        name="mix_features",
    )(inner, cot, rows)


def gated(x_ref, mixed_ref, scale_ref, bias_ref):
    x = x_ref[...].astype(F32)
    mixed = mixed_ref[...].astype(F32)
    return x, mixed, 0.5 * jnp.tanh(0.5 * (x * scale_ref[...] + bias_ref[...])) + 0.5


def enter_kernel(x_ref, mixed_ref, scale_ref, bias_ref, panel_ref, hidden_ref, inner_ref):
    x, mixed, gate = gated(x_ref, mixed_ref, scale_ref, bias_ref)
    hidden_ref[...] = (x + gate * mixed).astype(BF16)
    for k in range(x_ref.shape[0]):
        inner = lax.dot_general(
            panel_ref[...],
            hidden_ref[k],
            (((1,), (1,)), ((), ())),
            preferred_element_type=F32,
        )
        inner_ref[k] = inner.astype(BF16)


def back_kernel(
    x_ref, mixed_ref, scale_ref, bias_ref, panel_ref, cot_ref, d_ref, d_mixed_ref, local_ref
):
    _, mixed, gate = gated(x_ref, mixed_ref, scale_ref, bias_ref)
    slope = 1.0 + scale_ref[...] * gate * (1.0 - gate) * mixed
    for k in range(x_ref.shape[0]):
        d_hidden = cot_ref[k].astype(F32) + lax.dot_general(
            d_ref[k],
            panel_ref[...],
            (((0,), (0,)), ((), ())),
            preferred_element_type=F32,
        )
        d_mixed_ref[k] = (d_hidden * gate[k]).astype(BF16)
        local_ref[k] = (d_hidden * slope[k]).astype(BF16)


def by_rows(kernel, x, mixed, scale, bias, panel, more, outs):
    owners, _, width = x.shape
    here = 4

    def spec(shape):
        return pl.BlockSpec((here,) + shape[1:], lambda g: (g, 0, 0))

    vector = pl.BlockSpec((1, width), lambda g: (0, 0))
    return pl.pallas_call(
        kernel,
        out_shape=outs,
        grid=(owners // here,),
        in_specs=[spec(x.shape), spec(x.shape), vector, vector]
        + [pl.BlockSpec((width, width), lambda g: (0, 0))]
        + [spec(m.shape) for m in more],
        out_specs=tuple(spec(o.shape) for o in outs),
    )(x, mixed, scale.reshape(1, width), bias.reshape(1, width), panel, *more)


def close_kernel(at_ref, d_ref, own_ref, x_ref, prod_ref, *more_refs):
    *part_refs, total = more_refs
    step, (owners, here, offs, width) = pl.program_id(0), d_ref.shape
    height = owners * offs
    d_wide = jnp.concatenate([d_ref[:, k].reshape(height, width) for k in range(here)], axis=1)
    x_wide = jnp.concatenate([x_ref[k] for k in range(here)], axis=1)
    more = lax.dot_general(
        d_wide, x_wide, (((1,), (1,)), ((), ())), preferred_element_type=F32
    )
    part = lax.dot_general(
        own_ref[...], d_wide, (((0,), (0,)), ((), ())), preferred_element_type=F32
    ).astype(BF16)
    for r, part_ref in enumerate(part_refs):

        @pl.when(step ^ at_ref[0] == r)
        def _(part_ref=part_ref):
            for k in range(here):
                part_ref[k] = part[:, k * width : (k + 1) * width]

    @pl.when(step == 0)
    def _():
        total[...] = more

    @pl.when(step > 0)
    def _():
        total[...] += more

    @pl.when(step == pl.num_programs(0) - 1)
    def _():
        prod_ref[...] = total[...].astype(BF16)


def close(at, d_first, own, x_plane):
    owners, plane, offs, width = d_first.shape
    height, here = owners * offs, lax.axis_size("c")
    steps_y = plane // here
    square = pl.BlockSpec((height, height), lambda g, at: (0, 0))
    part = jax.ShapeDtypeStruct((here, height, width), BF16)
    return pl.pallas_call(
        close_kernel,
        out_shape=(jax.ShapeDtypeStruct((height, height), BF16),) + (part,) * steps_y,
        grid_spec=pltpu.PrefetchScalarGridSpec(
            num_scalar_prefetch=1,
            grid=(steps_y,),
            in_specs=[
                pl.BlockSpec((owners, here, offs, width), lambda g, at: (0, g, 0, 0)),
                square,
                pl.BlockSpec((here, height, width), lambda g, at: (g, 0, 0)),
            ],
            out_specs=(square,)
            + (pl.BlockSpec(part.shape, lambda g, at: (0, 0, 0)),) * steps_y,
            scratch_shapes=[pltpu.VMEM((height, height), F32)],
        ),
        name="close",
    )(at, d_first, own, x_plane)


def finish_kernel(at_ref, crossed_ref, local_ref, *refs):
    *part_refs, out_ref = refs
    here = pl.program_id(0) ^ at_ref[0]
    crossed = crossed_ref[0, 0].astype(F32)
    for r, part_ref in enumerate(part_refs):

        @pl.when(here == r)
        def _(part_ref=part_ref):
            kept = part_ref[0].astype(F32)
            for c in range(local_ref.shape[1]):
                value = jnp.where(at_ref[1] == c, kept, crossed)
                out_ref[0, c] = (value + local_ref[0, c].astype(F32)).astype(BF16)


def finish(at, parts, crossed, local):
    here, height, width = parts[0].shape
    whole = pl.BlockSpec((1, here, height, width), lambda g, at: (g, 0, 0, 0))
    return pl.pallas_call(
        finish_kernel,
        out_shape=jax.ShapeDtypeStruct(local.shape, BF16),
        grid_spec=pltpu.PrefetchScalarGridSpec(
            num_scalar_prefetch=1,
            grid=(len(parts),),
            in_specs=[
                pl.BlockSpec((1, 1, height, width), lambda g, at: (g ^ at[0], 0, 0, 0)),
                whole,
            ]
            + [pl.BlockSpec((1, height, width), lambda g, at: (at[1], 0, 0))] * len(parts),
            out_specs=whole,
        ),
        name="finish",
    )(at, crossed, local, *parts)


def steps(
    tokens,
    cotangent,
    seq_first,
    seq_second,
    feat_first,
    feature_second_blocks,
    gate_scale,
    gate_bias,
):
    n_seq, n_hid = lax.axis_size(SEQ), lax.axis_size(HID)
    n_plane = lax.axis_size(PLANE)
    halves = n_hid // n_plane
    rows, width = tokens.shape
    blocks, block = seq_first.shape[0], seq_first.shape[1]
    offs, nb = seq_second.shape[0], seq_second.shape[1]
    groups, group = feat_first.shape[0], feat_first.shape[1]
    panels = feature_second_blocks.shape[1]
    count = rows // n_hid
    wide = (n_hid, count, width)
    tall = (n_hid, width, count)
    flat = (n_seq, offs, blocks, width)
    by_panel = (panels, group, count)

    x_blocks = tokens.reshape(blocks, block, width)
    first = dot("qkj,qjc->kqc", seq_first, x_blocks).astype(BF16).reshape(flat)
    first = move(first, SEQ)

    x_rows = x_blocks.transpose(1, 0, 2).reshape(wide)
    cot_rows = cotangent.reshape(blocks, block, width).transpose(1, 0, 2).reshape(wide)
    small = feature_second_blocks.reshape(-1, width)
    sent = cot_rows.transpose(0, 2, 1)
    eye = jnp.eye(groups, dtype=BF16)
    panel = (feat_first[:, :, None, :] * eye[:, None, :, None]).reshape(width, width)
    got = swap(sent, HID)
    x_plane = swap(x_blocks, PLANE)
    cot_moved = got.reshape(by_panel)
    for axis in ("c", "y", "zh"):
        small = gather(small, axis)
    second_all = small.reshape(group, panels, panels)

    strided = first.transpose(1, 0, 2, 3).reshape(offs, nb, width)
    mixed_j = dot("jab,jbc->jac", seq_second, strided).astype(BF16)
    mixed_j = mixed_j.reshape(offs, n_seq, blocks, width).transpose(1, 0, 2, 3)
    mixed = move(mixed_j, SEQ).reshape(wide)
    hidden, inner = by_rows(
        enter_kernel,
        x_rows,
        mixed,
        gate_scale,
        gate_bias,
        panel,
        (),
        (jax.ShapeDtypeStruct(wide, BF16), jax.ShapeDtypeStruct(tall, BF16)),
    )
    inner_moved = move(inner, HID).reshape(by_panel)
    outer, d_inner = mix_features(inner_moved, cot_moved, second_all)
    d_back = move(d_inner.reshape(tall), HID)
    outer = swap(outer.reshape(tall), HID).transpose(0, 2, 1)
    d_mixed, local = by_rows(
        back_kernel,
        x_rows,
        mixed,
        gate_scale,
        gate_bias,
        panel,
        (cot_rows, d_back),
        (jax.ShapeDtypeStruct(wide, BF16), jax.ShapeDtypeStruct(wide, BF16)),
    )
    d_mixed = move(d_mixed.reshape(flat), SEQ)
    d_mixed_j = d_mixed.transpose(1, 0, 2, 3).reshape(offs, nb, width)
    d_first_j = dot("jab,jac->jbc", seq_second, d_mixed_j).astype(BF16)
    d_first_j = d_first_j.reshape(offs, n_seq * blocks, width).transpose(1, 0, 2)
    d_first = move(d_first_j, SEQ + PLANE).reshape(n_seq, n_plane, offs, width)

    part = dot("jac,jbc->jab", d_mixed_j, strided).astype(BF16)
    part = part.reshape(offs, halves, n_plane, nb // n_hid, nb).transpose(2, 1, 0, 3, 4)
    part = part.reshape((lax.axis_size("y"), lax.axis_size("c")) + part.shape[1:])
    part = fold(part, "c", 1).astype(BF16)
    part = fold(part, "y", 0)
    second_grad = fold(part, "zh", 0)

    own = lax.dynamic_index_in_dim(seq_first, lax.axis_index(PLANE), 0, keepdims=False)
    at = jnp.stack([lax.axis_index("y"), lax.axis_index("c")]).astype(jnp.int32)
    prod, *parts = close(at, d_first, own, x_plane)
    near = lax.axis_size("y")
    for r in range(1, near):
        parts[r] = lax.ppermute(parts[r], "y", [(k, k ^ r) for k in range(near)])
    crossed = jnp.stack([lax.dynamic_index_in_dim(p, 1 - at[1], 0, keepdims=True) for p in parts])
    crossed = lax.ppermute(crossed, "c", [(0, 1), (1, 0)])
    prod = move(prod.reshape(n_hid, offs, block), HID)
    first_grad = prod.reshape(halves, n_plane, offs, block).astype(F32).sum(0)

    def whole(value):
        return value.reshape(block, blocks, width).transpose(1, 0, 2).reshape(rows, width)

    result = whole((hidden.astype(F32) + outer.astype(F32)).astype(BF16))
    local = whole(local)
    local = local.reshape(near, len(at), block, width)
    token_grad = finish(at, parts, crossed, local).reshape(rows, width)
    return result, token_grad, first_grad, second_grad


def solution(mesh):
    fine = Mesh(mesh.devices.reshape(4, 4, 2, 4, 2), ("zl", "x", "zh", "y", "c"))
    return jax.shard_map(
        steps,
        mesh=fine,
        in_specs=(
            P(SEQ, HID),
            P(SEQ, HID),
            P(SEQ, None, None),
            P(SEQ, None, None),
            P(HID, None, None),
            P(HID, None, None),
            P(HID),
            P(HID),
        ),
        out_specs=(P(SEQ, HID), P(SEQ, HID), P(SEQ, HID, None), P(SEQ, HID, None)),
        check_vma=False,
    )
```

```python
import jax
import jax.numpy as jnp
from jax import lax
from jax.experimental import pallas as pl
from jax.experimental.pallas import tpu as pltpu
from jax.sharding import Mesh
from jax.sharding import PartitionSpec as P

SEQ = ("zl", "x")
HID = ("zh", "y", "c")
PLANE = ("y", "c")
F32 = jnp.float32
BF16 = jnp.bfloat16


def move(value, axes):
    return lax.all_to_all(value, axes, split_axis=0, concat_axis=0, tiled=True)


def trade(value, axis, dim):
    size, me = lax.axis_size(axis), lax.axis_index(axis)
    parts = [
        lax.dynamic_index_in_dim(value, me ^ r, dim, keepdims=True) for r in range(1, size)
    ]
    if size > 2:
        parts = lax.optimization_barrier(parts)
    got = []
    for r in range(1, size):
        got.append(lax.ppermute(parts[r - 1], axis, [(s, s ^ r) for s in range(size)]))
    return got


def fold(value, axis, dim):
    got = trade(value, axis, dim)
    total = lax.dynamic_index_in_dim(value, lax.axis_index(axis), dim).astype(F32)
    for part in got:
        total = total + part.astype(F32)
    return total.squeeze(dim)


def gather(value, axis):
    size, me = lax.axis_size(axis), lax.axis_index(axis)
    whole = jnp.zeros((size,) + value.shape, value.dtype)
    whole = lax.dynamic_update_index_in_dim(whole, value, me, 0)
    for r in range(1, size):
        other = lax.ppermute(value, axis, [(s, s ^ r) for s in range(size)])
        whole = lax.dynamic_update_index_in_dim(whole, other, me ^ r, 0)
    return whole


def turn(value, axis, dim):
    size, me = lax.axis_size(axis), lax.axis_index(axis)
    got = trade(value, axis, dim)
    for r in range(1, size):
        value = lax.dynamic_update_slice_in_dim(value, got[r - 1], me ^ r, dim)
    return value


def swap(value, axes):
    shape = value.shape
    value = value.reshape(tuple(lax.axis_size(a) for a in axes) + shape[1:])
    for dim, axis in enumerate(axes):
        value = turn(value, axis, dim)
    return value.reshape(shape)


def dot(spec, left, right):
    return jnp.einsum(spec, left, right, preferred_element_type=F32)


def mix_kernel(inner_ref, cot_ref, rows_ref, outer_ref, d_inner_ref):
    panels, here, count = inner_ref.shape
    offs = 16
    width = panels * offs
    col = lax.broadcasted_iota(jnp.int32, (panels, width), 1)
    row = lax.broadcasted_iota(jnp.int32, (panels, width), 0)
    pick = (col // offs == row).astype(F32).astype(BF16)
    at = lax.broadcasted_iota(jnp.int32, (width, width), 0) % offs
    to = lax.broadcasted_iota(jnp.int32, (width, width), 1) % offs
    for k in range(0, here, offs):
        part = pl.ds(k, offs)
        rows = rows_ref[:, part].reshape(width, panels)
        full = jnp.dot(rows, pick, preferred_element_type=F32)
        spread = jnp.where(at == to, full, 0.0).astype(BF16)
        cot = cot_ref[:, part].reshape(width, count)
        d_act = jnp.dot(spread, cot, preferred_element_type=F32)
        inner = inner_ref[:, part].reshape(width, count).astype(F32)
        cdf = 0.5 * (1.0 + lax.erf(inner * 0.7071067811865476))
        density = jnp.exp(-0.5 * inner * inner) * 0.3989422804014327
        d_inner = (d_act * (cdf + inner * density)).astype(BF16)
        d_inner_ref[:, part] = d_inner.reshape(panels, offs, count)
        act = (inner * cdf).astype(BF16)
        outer = lax.dot_general(
            spread, act, (((0,), (0,)), ((), ())), preferred_element_type=F32
        ).astype(BF16)
        outer_ref[:, part] = outer.reshape(panels, offs, count)


def mix_features(inner, cot, blocks):
    panels, group, count = inner.shape
    offs = 32
    rows = blocks.transpose(2, 0, 1)
    data = pl.BlockSpec((panels, offs, count), lambda g: (0, g, 0))
    return pl.pallas_call(
        mix_kernel,
        out_shape=(jax.ShapeDtypeStruct(inner.shape, BF16),) * 2,
        grid=(group // offs,),
        in_specs=[data, data, pl.BlockSpec((panels, offs, panels), lambda g: (0, g, 0))],
        out_specs=(data, data),
        name="mix_features",
    )(inner, cot, rows)


def gated(x_ref, mixed_ref, scale_ref, bias_ref):
    x = x_ref[...].astype(F32)
    mixed = mixed_ref[...].astype(F32)
    return x, mixed, 0.5 * jnp.tanh(0.5 * (x * scale_ref[...] + bias_ref[...])) + 0.5


def enter_kernel(x_ref, mixed_ref, scale_ref, bias_ref, panel_ref, hidden_ref, inner_ref):
    x, mixed, gate = gated(x_ref, mixed_ref, scale_ref, bias_ref)
    hidden_ref[...] = (x + gate * mixed).astype(BF16)
    for k in range(x_ref.shape[0]):
        inner = lax.dot_general(
            panel_ref[...],
            hidden_ref[k],
            (((1,), (1,)), ((), ())),
            preferred_element_type=F32,
        )
        inner_ref[k] = inner.astype(BF16)


def back_kernel(
    x_ref, mixed_ref, scale_ref, bias_ref, panel_ref, cot_ref, d_ref, d_mixed_ref, local_ref
):
    _, mixed, gate = gated(x_ref, mixed_ref, scale_ref, bias_ref)
    slope = 1.0 + scale_ref[...] * gate * (1.0 - gate) * mixed
    for k in range(x_ref.shape[0]):
        d_hidden = cot_ref[k].astype(F32) + lax.dot_general(
            d_ref[k],
            panel_ref[...],
            (((0,), (0,)), ((), ())),
            preferred_element_type=F32,
        )
        d_mixed_ref[k] = (d_hidden * gate[k]).astype(BF16)
        local_ref[k] = (d_hidden * slope[k]).astype(BF16)


def by_rows(kernel, x, mixed, scale, bias, panel, more, outs):
    owners, _, width = x.shape
    here = 8

    def spec(shape):
        return pl.BlockSpec((here,) + shape[1:], lambda g: (g, 0, 0))

    vector = pl.BlockSpec((1, width), lambda g: (0, 0))
    return pl.pallas_call(
        kernel,
        out_shape=outs,
        grid=(owners // here,),
        in_specs=[spec(x.shape), spec(x.shape), vector, vector]
        + [pl.BlockSpec((width, width), lambda g: (0, 0))]
        + [spec(m.shape) for m in more],
        out_specs=tuple(spec(o.shape) for o in outs),
    )(x, mixed, scale.reshape(1, width), bias.reshape(1, width), panel, *more)


def close_kernel(at_ref, d_ref, own_ref, x_ref, prod_ref, *more_refs):
    *part_refs, total = more_refs
    step, (owners, here, offs, width) = pl.program_id(0), d_ref.shape
    height = owners * offs
    d_wide = jnp.concatenate([d_ref[:, k].reshape(height, width) for k in range(here)], axis=1)
    x_wide = jnp.concatenate([x_ref[k] for k in range(here)], axis=1)
    more = lax.dot_general(
        d_wide, x_wide, (((1,), (1,)), ((), ())), preferred_element_type=F32
    )
    part = lax.dot_general(
        own_ref[...], d_wide, (((0,), (0,)), ((), ())), preferred_element_type=F32
    ).astype(BF16)
    cores = part_refs[0].shape[0]
    near = here // cores
    for i in range(near):
        for r, part_ref in enumerate(part_refs):

            @pl.when((step * near + i) ^ at_ref[0] == r)
            def _(i=i, part_ref=part_ref):
                for k in range(cores):
                    lane = (i * cores + k) * width
                    part_ref[k] = part[:, lane : lane + width]

    @pl.when(step == 0)
    def _():
        total[...] = more

    @pl.when(step > 0)
    def _():
        total[...] += more

    @pl.when(step == pl.num_programs(0) - 1)
    def _():
        prod_ref[...] = total[...].astype(BF16)


def close(at, d_first, own, x_plane):
    owners, plane, offs, width = d_first.shape
    height, here, cores = owners * offs, plane // 2, lax.axis_size("c")
    near = plane // cores
    square = pl.BlockSpec((height, height), lambda g, at: (0, 0))
    part = jax.ShapeDtypeStruct((cores, height, width), BF16)
    return pl.pallas_call(
        close_kernel,
        out_shape=(jax.ShapeDtypeStruct((height, height), BF16),) + (part,) * near,
        grid_spec=pltpu.PrefetchScalarGridSpec(
            num_scalar_prefetch=1,
            grid=(plane // here,),
            in_specs=[
                pl.BlockSpec((owners, here, offs, width), lambda g, at: (0, g, 0, 0)),
                square,
                pl.BlockSpec((here, height, width), lambda g, at: (g, 0, 0)),
            ],
            out_specs=(square,)
            + (pl.BlockSpec(part.shape, lambda g, at: (0, 0, 0)),) * near,
            scratch_shapes=[pltpu.VMEM((height, height), F32)],
        ),
        name="close",
    )(at, d_first, own, x_plane)


def finish_kernel(at_ref, crossed_ref, local_ref, *refs):
    *part_refs, out_ref = refs
    step, here = pl.program_id(0), local_ref.shape[0]
    for i in range(here):
        for r, part_ref in enumerate(part_refs):

            @pl.when((step * here + i) ^ at_ref[0] == r)
            def _(i=i, r=r, part_ref=part_ref):
                kept = part_ref[0].astype(F32)
                crossed = crossed_ref[r % here, 0].astype(F32)
                for c in range(local_ref.shape[1]):
                    value = jnp.where(at_ref[1] == c, kept, crossed)
                    out_ref[i, c] = (value + local_ref[i, c].astype(F32)).astype(BF16)


def finish(at, parts, crossed, local):
    cores, height, width = parts[0].shape
    here = 2
    whole = pl.BlockSpec((here, cores, height, width), lambda g, at: (g, 0, 0, 0))
    return pl.pallas_call(
        finish_kernel,
        out_shape=jax.ShapeDtypeStruct(local.shape, BF16),
        grid_spec=pltpu.PrefetchScalarGridSpec(
            num_scalar_prefetch=1,
            grid=(len(parts) // here,),
            in_specs=[
                pl.BlockSpec(
                    (here, 1, height, width), lambda g, at: (g ^ (at[0] // here), 0, 0, 0)
                ),
                whole,
            ]
            + [pl.BlockSpec((1, height, width), lambda g, at: (at[1], 0, 0))] * len(parts),
            out_specs=whole,
        ),
        name="finish",
    )(at, crossed, local, *parts)


def steps(
    tokens,
    cotangent,
    seq_first,
    seq_second,
    feat_first,
    feature_second_blocks,
    gate_scale,
    gate_bias,
):
    n_seq, n_hid = lax.axis_size(SEQ), lax.axis_size(HID)
    n_plane = lax.axis_size(PLANE)
    halves = n_hid // n_plane
    rows, width = tokens.shape
    blocks, block = seq_first.shape[0], seq_first.shape[1]
    offs, nb = seq_second.shape[0], seq_second.shape[1]
    groups, group = feat_first.shape[0], feat_first.shape[1]
    panels = feature_second_blocks.shape[1]
    count = rows // n_hid
    wide = (n_hid, count, width)
    tall = (n_hid, width, count)
    flat = (n_seq, offs, blocks, width)
    by_panel = (panels, group, count)

    x_blocks = tokens.reshape(blocks, block, width)
    first = dot("qkj,qjc->kqc", seq_first, x_blocks).astype(BF16).reshape(flat)
    first = move(first, SEQ)

    x_rows = x_blocks.transpose(1, 0, 2).reshape(wide)
    cot_rows = cotangent.reshape(blocks, block, width).transpose(1, 0, 2).reshape(wide)
    small = feature_second_blocks.reshape(-1, width)
    sent = cot_rows.transpose(0, 2, 1)
    eye = jnp.eye(groups, dtype=BF16)
    panel = (feat_first[:, :, None, :] * eye[:, None, :, None]).reshape(width, width)
    got = swap(sent, HID)
    x_plane = swap(x_blocks, PLANE)
    cot_moved = got.reshape(by_panel)
    for axis in ("c", "y", "zh"):
        small = gather(small, axis)
    second_all = small.reshape(group, panels, panels)

    strided = first.transpose(1, 0, 2, 3).reshape(offs, nb, width)
    mixed_j = dot("jab,jbc->jac", seq_second, strided).astype(BF16)
    mixed_j = mixed_j.reshape(offs, n_seq, blocks, width).transpose(1, 0, 2, 3)
    mixed = move(mixed_j, SEQ).reshape(wide)
    hidden, inner = by_rows(
        enter_kernel,
        x_rows,
        mixed,
        gate_scale,
        gate_bias,
        panel,
        (),
        (jax.ShapeDtypeStruct(wide, BF16), jax.ShapeDtypeStruct(tall, BF16)),
    )
    inner_moved = move(inner, HID).reshape(by_panel)
    outer, d_inner = mix_features(inner_moved, cot_moved, second_all)
    d_back = move(d_inner.reshape(tall), HID)
    outer = swap(outer.reshape(tall), HID).transpose(0, 2, 1)
    d_mixed, local = by_rows(
        back_kernel,
        x_rows,
        mixed,
        gate_scale,
        gate_bias,
        panel,
        (cot_rows, d_back),
        (jax.ShapeDtypeStruct(wide, BF16), jax.ShapeDtypeStruct(wide, BF16)),
    )
    d_mixed = move(d_mixed.reshape(flat), SEQ)
    d_mixed_j = d_mixed.transpose(1, 0, 2, 3).reshape(offs, nb, width)
    d_first_j = dot("jab,jac->jbc", seq_second, d_mixed_j).astype(BF16)
    d_first_j = d_first_j.reshape(offs, n_seq * blocks, width).transpose(1, 0, 2)
    d_first = move(d_first_j, SEQ + PLANE).reshape(n_seq, n_plane, offs, width)

    part = dot("jac,jbc->jab", d_mixed_j, strided).astype(BF16)
    part = part.reshape(offs, halves, n_plane, nb // n_hid, nb).transpose(2, 1, 0, 3, 4)
    part = part.reshape((lax.axis_size("y"), lax.axis_size("c")) + part.shape[1:])
    part = fold(part, "c", 1).astype(BF16)
    part = fold(part, "y", 0)
    second_grad = fold(part, "zh", 0)

    own = lax.dynamic_index_in_dim(seq_first, lax.axis_index(PLANE), 0, keepdims=False)
    at = jnp.stack([lax.axis_index("y"), lax.axis_index("c")]).astype(jnp.int32)
    prod, *parts = close(at, d_first, own, x_plane)
    near = lax.axis_size("y")
    for r in range(1, near):
        parts[r] = lax.ppermute(parts[r], "y", [(k, k ^ r) for k in range(near)])
    crossed = jnp.stack([lax.dynamic_index_in_dim(p, 1 - at[1], 0, keepdims=True) for p in parts])
    crossed = lax.ppermute(crossed, "c", [(0, 1), (1, 0)])
    prod = move(prod.reshape(n_hid, offs, block), HID)
    first_grad = prod.reshape(halves, n_plane, offs, block).astype(F32).sum(0)

    def whole(value):
        return value.reshape(block, blocks, width).transpose(1, 0, 2).reshape(rows, width)

    result = whole((hidden.astype(F32) + outer.astype(F32)).astype(BF16))
    local = whole(local)
    local = local.reshape(near, len(at), block, width)
    token_grad = finish(at, parts, crossed, local).reshape(rows, width)
    return result, token_grad, first_grad, second_grad


def solution(mesh):
    fine = Mesh(mesh.devices.reshape(4, 4, 2, 4, 2), ("zl", "x", "zh", "y", "c"))
    return jax.shard_map(
        steps,
        mesh=fine,
        in_specs=(
            P(SEQ, HID),
            P(SEQ, HID),
            P(SEQ, None, None),
            P(SEQ, None, None),
            P(HID, None, None),
            P(HID, None, None),
            P(HID),
            P(HID),
        ),
        out_specs=(P(SEQ, HID), P(SEQ, HID), P(SEQ, HID, None), P(SEQ, HID, None)),
        check_vma=False,
    )
```

```python
import jax
import jax.numpy as jnp
from jax import lax
from jax.experimental import pallas as pl
from jax.experimental.pallas import tpu as pltpu
from jax.sharding import Mesh
from jax.sharding import PartitionSpec as P

SEQ = ("zl", "x")
HID = ("zh", "y", "c")
PLANE = ("y", "c")
F32 = jnp.float32
BF16 = jnp.bfloat16


def move(value, axes):
    return lax.all_to_all(value, axes, split_axis=0, concat_axis=0, tiled=True)


def trade(value, axis, dim):
    size, me = lax.axis_size(axis), lax.axis_index(axis)
    parts = [
        lax.dynamic_index_in_dim(value, me ^ r, dim, keepdims=True) for r in range(1, size)
    ]
    if size > 2:
        parts = lax.optimization_barrier(parts)
    got = []
    for r in range(1, size):
        got.append(lax.ppermute(parts[r - 1], axis, [(s, s ^ r) for s in range(size)]))
    return got


def fold(value, axis, dim):
    got = trade(value, axis, dim)
    total = lax.dynamic_index_in_dim(value, lax.axis_index(axis), dim).astype(F32)
    for part in got:
        total = total + part.astype(F32)
    return total.squeeze(dim)


def gather(value, axis):
    size, me = lax.axis_size(axis), lax.axis_index(axis)
    whole = jnp.zeros((size,) + value.shape, value.dtype)
    whole = lax.dynamic_update_index_in_dim(whole, value, me, 0)
    for r in range(1, size):
        other = lax.ppermute(value, axis, [(s, s ^ r) for s in range(size)])
        whole = lax.dynamic_update_index_in_dim(whole, other, me ^ r, 0)
    return whole


def turn(value, axis, dim):
    size, me = lax.axis_size(axis), lax.axis_index(axis)
    got = trade(value, axis, dim)
    for r in range(1, size):
        value = lax.dynamic_update_slice_in_dim(value, got[r - 1], me ^ r, dim)
    return value


def swap(value, axes):
    shape = value.shape
    value = value.reshape(tuple(lax.axis_size(a) for a in axes) + shape[1:])
    for dim, axis in enumerate(axes):
        value = turn(value, axis, dim)
    return value.reshape(shape)


def dot(spec, left, right):
    return jnp.einsum(spec, left, right, preferred_element_type=F32)


def mix_kernel(inner_ref, cot_ref, rows_ref, outer_ref, d_inner_ref):
    panels, here, count = inner_ref.shape
    offs = 16
    width = panels * offs
    col = lax.broadcasted_iota(jnp.int32, (panels, width), 1)
    row = lax.broadcasted_iota(jnp.int32, (panels, width), 0)
    pick = (col // offs == row).astype(F32).astype(BF16)
    at = lax.broadcasted_iota(jnp.int32, (width, width), 0) % offs
    to = lax.broadcasted_iota(jnp.int32, (width, width), 1) % offs
    for k in range(0, here, offs):
        part = pl.ds(k, offs)
        rows = rows_ref[:, part].reshape(width, panels)
        full = jnp.dot(rows, pick, preferred_element_type=F32)
        spread = jnp.where(at == to, full, 0.0).astype(BF16)
        cot = cot_ref[:, part].reshape(width, count)
        d_act = jnp.dot(spread, cot, preferred_element_type=F32)
        inner = inner_ref[:, part].reshape(width, count).astype(F32)
        cdf = 0.5 * (1.0 + lax.erf(inner * 0.7071067811865476))
        density = jnp.exp(-0.5 * inner * inner) * 0.3989422804014327
        d_inner = (d_act * (cdf + inner * density)).astype(BF16)
        d_inner_ref[:, part] = d_inner.reshape(panels, offs, count)
        act = (inner * cdf).astype(BF16)
        outer = lax.dot_general(
            spread, act, (((0,), (0,)), ((), ())), preferred_element_type=F32
        ).astype(BF16)
        outer_ref[:, part] = outer.reshape(panels, offs, count)


def mix_features(inner, cot, blocks):
    panels, group, count = inner.shape
    offs = 32
    rows = blocks.transpose(2, 0, 1)
    data = pl.BlockSpec((panels, offs, count), lambda g: (0, g, 0))
    return pl.pallas_call(
        mix_kernel,
        out_shape=(jax.ShapeDtypeStruct(inner.shape, BF16),) * 2,
        grid=(group // offs,),
        in_specs=[data, data, pl.BlockSpec((panels, offs, panels), lambda g: (0, g, 0))],
        out_specs=(data, data),
        name="mix_features",
    )(inner, cot, rows)


def gated(x_ref, mixed_ref, scale_ref, bias_ref):
    x = x_ref[...].astype(F32)
    mixed = mixed_ref[...].astype(F32)
    return x, mixed, 0.5 * jnp.tanh(0.5 * (x * scale_ref[...] + bias_ref[...])) + 0.5


def enter_kernel(x_ref, mixed_ref, scale_ref, bias_ref, panel_ref, hidden_ref, inner_ref):
    x, mixed, gate = gated(x_ref, mixed_ref, scale_ref, bias_ref)
    hidden_ref[...] = (x + gate * mixed).astype(BF16)
    for k in range(x_ref.shape[0]):
        inner = lax.dot_general(
            panel_ref[...],
            hidden_ref[k],
            (((1,), (1,)), ((), ())),
            preferred_element_type=F32,
        )
        inner_ref[k] = inner.astype(BF16)


def back_kernel(
    x_ref, mixed_ref, scale_ref, bias_ref, panel_ref, cot_ref, d_ref, d_mixed_ref, local_ref
):
    _, mixed, gate = gated(x_ref, mixed_ref, scale_ref, bias_ref)
    slope = 1.0 + scale_ref[...] * gate * (1.0 - gate) * mixed
    for k in range(x_ref.shape[0]):
        d_hidden = cot_ref[k].astype(F32) + lax.dot_general(
            d_ref[k],
            panel_ref[...],
            (((0,), (0,)), ((), ())),
            preferred_element_type=F32,
        )
        d_mixed_ref[k] = (d_hidden * gate[k]).astype(BF16)
        local_ref[k] = (d_hidden * slope[k]).astype(BF16)


def by_rows(kernel, x, mixed, scale, bias, panel, more, outs):
    owners, _, width = x.shape
    here = 8

    def spec(shape):
        return pl.BlockSpec((here,) + shape[1:], lambda g: (g, 0, 0))

    vector = pl.BlockSpec((1, width), lambda g: (0, 0))
    return pl.pallas_call(
        kernel,
        out_shape=outs,
        grid=(owners // here,),
        in_specs=[spec(x.shape), spec(x.shape), vector, vector]
        + [pl.BlockSpec((width, width), lambda g: (0, 0))]
        + [spec(m.shape) for m in more],
        out_specs=tuple(spec(o.shape) for o in outs),
    )(x, mixed, scale.reshape(1, width), bias.reshape(1, width), panel, *more)


def close_kernel(at_ref, d_ref, own_ref, x_ref, prod_ref, *more_refs):
    *part_refs, total = more_refs
    step, (owners, here, offs, width) = pl.program_id(0), d_ref.shape
    height = owners * offs
    d_wide = jnp.concatenate([d_ref[:, k].reshape(height, width) for k in range(here)], axis=1)
    x_wide = jnp.concatenate([x_ref[k] for k in range(here)], axis=1)
    more = lax.dot_general(
        d_wide, x_wide, (((1,), (1,)), ((), ())), preferred_element_type=F32
    )
    part = lax.dot_general(
        own_ref[...], d_wide, (((0,), (0,)), ((), ())), preferred_element_type=F32
    ).astype(BF16)
    cores = part_refs[0].shape[0]
    near = here // cores
    for i in range(near):
        for r, part_ref in enumerate(part_refs):

            @pl.when((step * near + i) ^ at_ref[0] == r)
            def _(i=i, part_ref=part_ref):
                for k in range(cores):
                    lane = (i * cores + k) * width
                    part_ref[k] = part[:, lane : lane + width]

    @pl.when(step == 0)
    def _():
        total[...] = more

    @pl.when(step > 0)
    def _():
        total[...] += more

    @pl.when(step == pl.num_programs(0) - 1)
    def _():
        prod_ref[...] = total[...].astype(BF16)


def close(at, d_first, own, x_plane):
    owners, plane, offs, width = d_first.shape
    height, here, cores = owners * offs, plane // 2, lax.axis_size("c")
    near = plane // cores
    square = pl.BlockSpec((height, height), lambda g, at: (0, 0))
    part = jax.ShapeDtypeStruct((cores, height, width), BF16)
    return pl.pallas_call(
        close_kernel,
        out_shape=(jax.ShapeDtypeStruct((height, height), BF16),) + (part,) * near,
        grid_spec=pltpu.PrefetchScalarGridSpec(
            num_scalar_prefetch=1,
            grid=(plane // here,),
            in_specs=[
                pl.BlockSpec((owners, here, offs, width), lambda g, at: (0, g, 0, 0)),
                square,
                pl.BlockSpec((here, height, width), lambda g, at: (g, 0, 0)),
            ],
            out_specs=(square,)
            + (pl.BlockSpec(part.shape, lambda g, at: (0, 0, 0)),) * near,
            scratch_shapes=[pltpu.VMEM((height, height), F32)],
        ),
        name="close",
    )(at, d_first, own, x_plane)


def finish_kernel(at_ref, crossed_ref, local_ref, *refs):
    *part_refs, out_ref = refs
    step, here = pl.program_id(0), local_ref.shape[0]
    for i in range(here):
        for r, part_ref in enumerate(part_refs):

            @pl.when((step * here + i) ^ at_ref[0] == r)
            def _(i=i, r=r, part_ref=part_ref):
                kept = part_ref[0].astype(F32)
                crossed = crossed_ref[r % here, 0].astype(F32)
                for c in range(local_ref.shape[1]):
                    value = jnp.where(at_ref[1] == c, kept, crossed)
                    out_ref[i, c] = (value + local_ref[i, c].astype(F32)).astype(BF16)


def finish(at, parts, crossed, local):
    cores, height, width = parts[0].shape
    here = 2
    whole = pl.BlockSpec((here, cores, height, width), lambda g, at: (g, 0, 0, 0))
    return pl.pallas_call(
        finish_kernel,
        out_shape=jax.ShapeDtypeStruct(local.shape, BF16),
        grid_spec=pltpu.PrefetchScalarGridSpec(
            num_scalar_prefetch=1,
            grid=(len(parts) // here,),
            in_specs=[
                pl.BlockSpec(
                    (here, 1, height, width), lambda g, at: (g ^ (at[0] // here), 0, 0, 0)
                ),
                whole,
            ]
            + [pl.BlockSpec((1, height, width), lambda g, at: (at[1], 0, 0))] * len(parts),
            out_specs=whole,
        ),
        name="finish",
    )(at, crossed, local, *parts)


def steps(
    tokens,
    cotangent,
    seq_first,
    seq_second,
    feat_first,
    feature_second_blocks,
    gate_scale,
    gate_bias,
):
    n_seq, n_hid = lax.axis_size(SEQ), lax.axis_size(HID)
    n_plane = lax.axis_size(PLANE)
    halves = n_hid // n_plane
    zh = lax.axis_index("zh")
    rows, width = tokens.shape
    blocks, block = seq_first.shape[0], seq_first.shape[1]
    offs, nb = seq_second.shape[0], seq_second.shape[1]
    groups, group = feat_first.shape[0], feat_first.shape[1]
    panels = feature_second_blocks.shape[1]
    count = rows // n_hid
    wide = (n_hid, count, width)
    tall = (n_hid, width, count)
    flat = (n_seq, offs, blocks, width)
    by_panel = (panels, group, count)

    x_blocks = tokens.reshape(blocks, block, width)
    first = dot("qkj,qjc->kqc", seq_first, x_blocks).astype(BF16).reshape(flat)
    first = move(first, SEQ)

    x_rows = x_blocks.transpose(1, 0, 2).reshape(wide)
    cot_rows = cotangent.reshape(blocks, block, width).transpose(1, 0, 2).reshape(wide)
    small = feature_second_blocks.reshape(-1, width)
    sent = cot_rows.transpose(0, 2, 1)
    eye = jnp.eye(groups, dtype=BF16)
    panel = (feat_first[:, :, None, :] * eye[:, None, :, None]).reshape(width, width)
    got = swap(sent, HID)
    x_plane = swap(x_blocks, PLANE)
    cot_moved = got.reshape(by_panel)
    for axis in ("c", "y", "zh"):
        small = gather(small, axis)
    second_all = small.reshape(group, panels, panels)

    strided = first.transpose(1, 0, 2, 3).reshape(offs, nb, width)
    mixed_j = dot("jab,jbc->jac", seq_second, strided).astype(BF16)
    mixed_j = mixed_j.reshape(offs, n_seq, blocks, width).transpose(1, 0, 2, 3)
    mixed = move(mixed_j, SEQ).reshape(wide)
    hidden, inner = by_rows(
        enter_kernel,
        x_rows,
        mixed,
        gate_scale,
        gate_bias,
        panel,
        (),
        (jax.ShapeDtypeStruct(wide, BF16), jax.ShapeDtypeStruct(tall, BF16)),
    )
    inner_moved = move(inner, HID).reshape(by_panel)
    outer, d_inner = mix_features(inner_moved, cot_moved, second_all)
    d_back = move(d_inner.reshape(tall), HID)
    outer = swap(outer.reshape(tall), HID).transpose(0, 2, 1)
    d_mixed, local = by_rows(
        back_kernel,
        x_rows,
        mixed,
        gate_scale,
        gate_bias,
        panel,
        (cot_rows, d_back),
        (jax.ShapeDtypeStruct(wide, BF16), jax.ShapeDtypeStruct(wide, BF16)),
    )
    d_mixed = move(d_mixed.reshape(flat), SEQ)
    d_mixed_j = d_mixed.transpose(1, 0, 2, 3).reshape(offs, nb, width)
    d_first_j = dot("jab,jac->jbc", seq_second, d_mixed_j).astype(BF16)
    d_first_j = d_first_j.reshape(offs, n_seq * blocks, width).transpose(1, 0, 2)
    d_first = move(d_first_j, SEQ + PLANE).reshape(n_seq, n_plane, offs, width)

    part = dot("jac,jbc->jab", d_mixed_j, strided).astype(BF16)
    part = part.reshape(offs, halves, n_plane, nb // n_hid, nb).transpose(2, 1, 0, 3, 4)
    part = part.reshape((lax.axis_size("y"), lax.axis_size("c")) + part.shape[1:])
    part = fold(part, "c", 1).astype(BF16)
    part = fold(part, "y", 0)
    keep = lax.dynamic_index_in_dim(part, zh, 0, keepdims=False)
    send = lax.dynamic_index_in_dim(part, 1 - zh, 0, keepdims=False).astype(BF16)
    second_grad = keep + lax.ppermute(send, "zh", [(0, 1), (1, 0)]).astype(F32)

    own = lax.dynamic_index_in_dim(seq_first, lax.axis_index(PLANE), 0, keepdims=False)
    at = jnp.stack([lax.axis_index("y"), lax.axis_index("c")]).astype(jnp.int32)
    prod, *parts = close(at, d_first, own, x_plane)
    near = lax.axis_size("y")
    for r in range(1, near):
        parts[r] = lax.ppermute(parts[r], "y", [(k, k ^ r) for k in range(near)])
    crossed = jnp.stack([lax.dynamic_index_in_dim(p, 1 - at[1], 0, keepdims=True) for p in parts])
    crossed = lax.ppermute(crossed, "c", [(0, 1), (1, 0)])
    prod = move(prod.reshape(n_hid, offs, block), HID)
    first_grad = prod.reshape(halves, n_plane, offs, block).astype(F32).sum(0)

    def whole(value):
        return value.reshape(block, blocks, width).transpose(1, 0, 2).reshape(rows, width)

    result = whole((hidden.astype(F32) + outer.astype(F32)).astype(BF16))
    local = whole(local)
    local = local.reshape(near, len(at), block, width)
    token_grad = finish(at, parts, crossed, local).reshape(rows, width)
    return result, token_grad, first_grad, second_grad


def solution(mesh):
    fine = Mesh(mesh.devices.reshape(4, 4, 2, 4, 2), ("zl", "x", "zh", "y", "c"))
    return jax.shard_map(
        steps,
        mesh=fine,
        in_specs=(
            P(SEQ, HID),
            P(SEQ, HID),
            P(SEQ, None, None),
            P(SEQ, None, None),
            P(HID, None, None),
            P(HID, None, None),
            P(HID),
            P(HID),
        ),
        out_specs=(P(SEQ, HID), P(SEQ, HID), P(SEQ, HID, None), P(SEQ, HID, None)),
        check_vma=False,
    )
```
